256 devices in a mesh: ctx: 16 (over x_lo, z), head: 16 (over x_hi, y, core).
Axes of the slice: x: 4 (x_hi: 2, x_lo: 2; x = x_hi * 2 + x_lo), y: 4, z: 8, core: 2. Of those that a mesh axis runs over, the one named last changes fastest.
Arguments:
- query: bfloat16 [4096, 8192], P('ctx', 'head'), may hold values from -6 to 6
- keyval: bfloat16 [4096, 2048], P('ctx'), may hold values from -6 to 6
- grad_out: bfloat16 [4096, 8192], P('ctx', 'head'), may hold values from -6 to 6
- vis_blocks: int32 [32, 24], replicated, may hold values from 0 to 31, as said below
- vis_count: int32 [32], replicated, may hold values from 1 to 24, as said below
- segment_ids: int32 [4096], replicated, may hold values from 0 to 31, never falling along the last dimension, each value on 1 to 256 neighbouring positions
- block_order: int32 [32], replicated, may hold values from 0 to 31, as said below
Outputs:
- attn_out: bfloat16 [4096, 8192], P('ctx', 'head')
- grad_query: bfloat16 [4096, 8192], P('ctx', 'head')
- grad_keyval: float32 [4096, 2048], P('ctx')
The draws below stay inside these ranges and needn't reach their ends.
Inputs may be any that keep to these rules, and one draw needn't show every extreme that they name: `vis_blocks`: row b lists in rising order the blocks that block b's queries may see (block 0 and b itself always among them), then repeats b up to 24 entries. `vis_count`: the number of listed blocks of each row; some row lists exactly 24. `block_order`: storage blocks 2 i and 2 i + 1 hold visibility blocks p and 31 - p for some p; every block is held once. `segment_ids`: segment numbers never fall along the tokens in visibility-block order.
All inputs are finite; a program needn't handle non-finite values.
Results may differ from the reference program's by a relative error of at most 0.025.
Values may be sent and summed in bfloat16 or wider, within the bound.
No kernel may reach another device: no remote copies, remote signals or barrier semaphores. Data moves between devices by JAX's collectives and lax.ppermute only.
A program may use at most 64 MiB of HBM per device.

```python
import math
import jax
import jax.numpy as jnp
import numpy as np
from jax import lax

QH = 64
KVH = 8
HD = 128
BLK = 128
NB = 32
MAXVIS = 24
TOKENS = 4096


def pair_order(key):
    pair_total = NB // 2
    picked = jax.random.permutation(jax.random.fold_in(key, 11), pair_total).astype(jnp.int32)
    flip_bits = jax.random.randint(jax.random.fold_in(key, 12), (pair_total,), 0, 2)
    first_ids = jnp.where(flip_bits == 1, NB - 1 - picked, picked)
    return jnp.stack([first_ids, NB - 1 - first_ids], axis=1).reshape(NB).astype(jnp.int32)


def visibility(key):
    shared = jax.random.randint(jax.random.fold_in(key, 21), (), NB // 8, NB // 2 + 1)
    prompt = jax.random.randint(jax.random.fold_in(key, 22), (), 1, shared)
    long_len = MAXVIS - shared
    short_len = NB - MAXVIS
    chosen_long = jax.random.randint(jax.random.fold_in(key, 23), (), 0, 2)
    chosen_len = jnp.where(chosen_long == 1, long_len, short_len)
    coin_bits = jax.random.randint(jax.random.fold_in(key, 24), (NB, NB), 0, 2)
    row_ids = jnp.arange(NB, dtype=jnp.int32)[:, None]
    col_ids = jnp.arange(NB, dtype=jnp.int32)[None, :]
    causal = col_ids <= row_ids
    in_prompt = row_ids < prompt
    in_tool = (row_ids >= prompt) & (row_ids < shared)
    in_chosen = (row_ids >= shared) & (row_ids < shared + chosen_len)
    in_rejected = row_ids >= shared + chosen_len
    tool_seen = (col_ids < prompt) | (col_ids == row_ids) | (col_ids >= prompt) & (coin_bits == 1)
    rejected_seen = (col_ids < shared) | (col_ids >= shared + chosen_len)
    seen = causal & (in_prompt | in_tool & tool_seen | in_chosen | in_rejected & rejected_seen)
    counts = jnp.sum(seen.astype(jnp.int32), axis=1).astype(jnp.int32)
    order_key = jnp.where(seen, col_ids, NB + col_ids)
    ranked = jnp.argsort(order_key, axis=1)[:, :MAXVIS].astype(jnp.int32)
    slot_ids = jnp.arange(MAXVIS, dtype=jnp.int32)[None, :]
    listed = jnp.where(slot_ids < counts[:, None], ranked, row_ids).astype(jnp.int32)
    return (listed, counts)


def draw_block_order(key, part):
    return pair_order(key)


def draw_vis_blocks(key, part):
    return visibility(key)[0]


def draw_vis_count(key, part):
    return visibility(key)[1]


def draw_query(key, part):
    own_key = jax.random.fold_in(key, 41)
    drawn = jnp.clip(jax.random.normal(jax.random.fold_in(own_key, 1), (TOKENS, QH * HD), jnp.float32), -6.0, 6.0)
    return drawn.astype(jnp.bfloat16)


def draw_keyval(key, part):
    own_key = jax.random.fold_in(key, 51)
    width_all = KVH * 2 * HD
    drawn = jnp.clip(jax.random.normal(jax.random.fold_in(own_key, 1), (TOKENS, width_all), jnp.float32), -6.0, 6.0)
    return drawn.astype(jnp.bfloat16)


def steps_of(rng, shape, shards, least, high):
    def one(position, shards_of):
        draws = jax.random.uniform(jax.random.fold_in(jax.random.fold_in(rng, 6), position), (shards_of,), jnp.float32, least / len(shards), high / len(shards))
        return jnp.repeat(jnp.exp(draws), shape[position] // shards_of).reshape((-1,) + (1,) * (len(shape) - position - 1))

    level = one(*shards[0])
    for cut in shards[1:]:
        level = level * one(*cut)
    return level


def split_up(amount, total, limit, slope):
    weights = [(1 << 20) // math.isqrt(rank ** slope) + 1 for rank in range(2, amount + 1)]
    surplus, holding = total - limit - (amount - 1), [1] * (amount - 1)
    while surplus > 0:
        candidates = [i for i in range(amount - 1) if holding[i] < limit]
        mass, remaining = sum([weights[i] for i in candidates]), surplus
        for i in candidates:
            addition = min(limit - holding[i], max(1, remaining * weights[i] // mass), surplus)
            holding[i] = holding[i] + addition
            surplus = surplus - addition
    return np.array([limit] + holding)


def ragged_sizes(rng, number_of, total, reach, slope):
    if number_of == 2:
        one = jax.random.randint(rng, (), max(1, total - reach), min(reach, total - 1) + 1)
        return jnp.stack([one, total - one])
    sizes = jnp.asarray(split_up(number_of, total, reach, slope), jnp.int32)
    couples = (number_of - 1) // 2
    donor, sink = sizes[1:1 + 2 * couples:2], sizes[2:2 + 2 * couples:2]
    margin = jnp.minimum(donor - 1, reach - sink)
    passed = jax.random.randint(jax.random.fold_in(rng, 1), (couples,), 0, 1 << 20) % (margin + 1)
    sizes = sizes.at[1:1 + 2 * couples:2].set(donor - passed).at[2:2 + 2 * couples:2].set(sink + passed)
    return sizes[jax.random.permutation(jax.random.fold_in(rng, 2), number_of)]


def bell_draw(key, shape, scale, limit, cuts=(), kind=jnp.bfloat16):
    array = scale * jax.random.normal(key, shape, jnp.float32)
    if cuts:
        array = array * steps_of(key, shape, cuts, -0.22, 0.18)
    return jnp.clip(array, -limit, limit).astype(kind)


def setup_inputs(seed: int = 0) -> dict:
    streams_of = jax.random.split(jax.random.key(seed), 8)
    return {
        "query": draw_query(jax.random.fold_in(streams_of[7], 71), 0),
        "keyval": draw_keyval(jax.random.fold_in(streams_of[7], 71), 0),
        "grad_out": bell_draw(streams_of[2], (TOKENS, QH * HD), 1.0, 6.0, ((0, 16), (1, 16))),
        "vis_blocks": draw_vis_blocks(jax.random.fold_in(streams_of[7], 71), 0),
        "vis_count": draw_vis_count(jax.random.fold_in(streams_of[7], 71), 0),
        "segment_ids": jnp.searchsorted(jnp.cumsum(ragged_sizes(streams_of[5], NB, TOKENS, 2 * BLK, 2)), jnp.arange(TOKENS), side="right").astype(jnp.int32),
        "block_order": draw_block_order(jax.random.fold_in(streams_of[7], 71), 0),
    }


very_negative = -1.0e30


def reference(query, keyval, grad_out, vis_blocks, vis_count, segment_ids, block_order):
    group_size = QH // KVH
    score_scale = HD ** -0.5
    highest = lax.Precision.HIGHEST
    positions = jnp.arange(NB, dtype=jnp.int32)
    inverse = jnp.sum(jnp.where(block_order[None, :] == positions[:, None], positions[None, :], 0), axis=1).astype(jnp.int32)
    query_pack = query.reshape(NB, BLK, KVH, group_size, HD)[inverse]
    keyval_pack = keyval.reshape(NB, BLK, KVH, 2, HD)[inverse]
    grad_pack = grad_out.reshape(NB, BLK, KVH, group_size, HD)[inverse]
    segment_pack = segment_ids.reshape(NB, BLK)
    token_pos = jnp.arange(BLK, dtype=jnp.int32)
    lower_part = token_pos[None, :] <= token_pos[:, None]
    slot_pos = jnp.arange(MAXVIS, dtype=jnp.int32)

    def one_block(dkv_acc, block_id):
        listed = vis_blocks[block_id]
        count_here = vis_count[block_id]
        q_here = query_pack[block_id].astype(jnp.float32)
        g_here = grad_pack[block_id].astype(jnp.float32)
        seg_here = segment_pack[block_id]
        intra = lower_part & (seg_here[:, None] == seg_here[None, :])
        valid = slot_pos < count_here
        own_slot = listed == block_id
        seen = valid[:, None, None] & (jnp.logical_not(own_slot)[:, None, None] | intra[None, :, :])
        seen = jnp.transpose(seen, (1, 0, 2))[None, None]
        fetched = keyval_pack[listed].astype(jnp.float32)
        key_part = fetched[:, :, :, 0, :]
        value_part = fetched[:, :, :, 1, :]
        scores = jnp.einsum("qhgd,mkhd->hgqmk", q_here, key_part, precision=highest) * score_scale
        row_max = jnp.max(jnp.where(seen, scores, very_negative), axis=(3, 4), keepdims=True)
        row_sum = jnp.sum(jnp.where(seen, jnp.exp(scores - row_max), 0.0), axis=(3, 4), keepdims=True)
        log_total = row_max + jnp.log(row_sum)
        weights = jnp.where(seen, jnp.exp(scores - log_total), 0.0)
        weights_low = lax.optimization_barrier(weights.astype(jnp.bfloat16)).astype(jnp.float32)
        out_here = jnp.einsum("hgqmk,mkhd->qhgd", weights_low, value_part, precision=highest).astype(jnp.bfloat16)
        out_wide = lax.optimization_barrier(out_here).astype(jnp.float32)
        delta = jnp.einsum("qhgd,qhgd->hgq", g_here, out_wide, precision=highest)
        grad_weights = jnp.einsum("qhgd,mkhd->hgqmk", g_here, value_part, precision=highest)
        grad_scores = (weights * (grad_weights - delta[:, :, :, None, None])).astype(jnp.bfloat16)
        grad_low = lax.optimization_barrier(grad_scores).astype(jnp.float32)
        dq_here = (jnp.einsum("hgqmk,mkhd->qhgd", grad_low, key_part, precision=highest) * score_scale).astype(jnp.bfloat16)
        dk_here = jnp.einsum("hgqmk,qhgd->mkhd", grad_low, q_here, precision=highest) * score_scale
        dv_here = jnp.einsum("hgqmk,qhgd->mkhd", weights_low, g_here, precision=highest)
        dkv_acc = dkv_acc.at[listed].add(jnp.stack([dk_here, dv_here], axis=3))
        return dkv_acc, (out_here, dq_here)

    start = jnp.zeros((NB, BLK, KVH, 2, HD), jnp.float32)
    dkv_pack, (out_pack, dq_pack) = lax.scan(one_block, start, positions)
    attn_out = out_pack[block_order].reshape(TOKENS, QH * HD)
    grad_query = dq_pack[block_order].reshape(TOKENS, QH * HD)
    grad_keyval = dkv_pack[block_order].reshape(TOKENS, KVH * 2 * HD)
    return attn_out, grad_query, grad_keyval
```

```python
import functools

import jax
import jax.numpy as jnp
from jax import lax
from jax.experimental import pallas as pl
from jax.experimental.pallas import tpu as pltpu
from jax.sharding import Mesh, PartitionSpec as P

QH = 64
KVH = 8
HD = 128
BLK = 128
NB = 32
HEADS = 4
ROWS = HEADS * BLK
SCALE = HD**-0.5
LOG2E = 1.4426950408889634
MASKED = -1e30
BF = jnp.bfloat16
F32 = jnp.float32
Z_SHIFTS = (4, 3, -3, 2, -2, 1, -1)
Y_SHIFTS = (2, 1, -1)


def shift(value, axis, size, by):
    return lax.ppermute(value, axis, [(i, (i + by) % size) for i in range(size)])


def swap(value, axis):
    return lax.ppermute(value, axis, [(0, 1), (1, 0)])


def nt(a, b):
    return lax.dot_general(a, b, (((1,), (1,)), ((), ())), preferred_element_type=F32)


def nn(a, b):
    return lax.dot_general(a, b, (((1,), (0,)), ((), ())), preferred_element_type=F32)


def tn(a, b):
    return lax.dot_general(a, b, (((0,), (0,)), ((), ())), preferred_element_type=F32)


def attention_kernel(
    ids, vis, count, order, q_ref, g_ref, seg_ref, *rest
):
    pieces = rest[: 2 * len(Z_SHIFTS) + 2]
    out_ref, dq_ref, mine_ref, other_ref = rest[len(pieces) : len(pieces) + 4]
    kv_scr, store, acc, inv, sem = rest[len(pieces) + 4 :]
    x, z, core = ids[0], ids[1], ids[4]
    n_piece = len(pieces) // 2
    shifts = (0,) + Z_SHIFTS

    def copies():
        out = []
        for p in range(2 * n_piece):
            which = core if p < n_piece else 1 - core
            source_z = lax.rem(z - shifts[p % n_piece] + 8, 8)
            for part in range(2):
                source_x = x if part == 0 else 1 - x
                out.append(
                    pltpu.make_async_copy(
                        pieces[p].at[pl.ds(part * 2 * BLK, 2 * BLK)],
                        kv_scr.at[which, source_x * 8 + source_z],
                        sem.at[2 * p + part],
                    )
                )
        return out

    for copy in copies():
        copy.start()

    def invert(j, carry):
        inv[order[j]] = j
        return carry

    lax.fori_loop(0, NB, invert, 0)
    acc[...] = jnp.zeros_like(acc)
    for copy in copies():
        copy.wait()

    own = x * 8 + z
    u_pos = lax.broadcasted_iota(jnp.int32, (BLK, BLK), 0)
    t_pos = lax.broadcasted_iota(jnp.int32, (BLK, BLK), 1)

    def kv(which, stored):
        return kv_scr[which, stored // 2, pl.ds(pl.multiple_of(lax.rem(stored, 2) * BLK, BLK), BLK), :]

    def own_block(i, carry):
        b = order[2 * own + i]
        n = count[b]
        at = pl.ds(pl.multiple_of(i * BLK, BLK), BLK)
        q = jnp.concatenate([q_ref[at, h * HD : (h + 1) * HD] for h in range(HEADS)], axis=0)
        g = jnp.concatenate([g_ref[at, h * HD : (h + 1) * HD] for h in range(HEADS)], axis=0)
        seg_t = jnp.broadcast_to(seg_ref[pl.ds(b, 1), :], (BLK, BLK))
        seg_u = jnp.transpose(seg_t)
        seen = (u_pos <= t_pos) & (seg_u == seg_t)
        seen = jnp.concatenate([seen.astype(F32)] * HEADS, axis=1) > 0.5

        def listed(s):
            v = vis[b, s]
            nxt = vis[b, jnp.minimum(s + 1, 23)]
            return inv[jnp.where(v < b, v, nxt)]

        def fold(fn, value):
            return functools.reduce(fn, [value[8 * r : 8 * r + 8] for r in range(value.shape[0] // 8)])

        diag = inv[b]
        scores = jnp.where(seen, nt(kv(0, diag), q), MASKED)
        store[0] = scores
        top = fold(jnp.maximum, scores)

        def score_pass(s, top):
            scores = nt(kv(0, listed(s)), q)
            store[s + 1] = scores
            return jnp.maximum(top, fold(jnp.maximum, scores))

        top = lax.fori_loop(0, n - 1, score_pass, top)
        top = jnp.max(top, axis=0, keepdims=True)

        def stored_at(s):
            return jnp.where(s == 0, diag, listed(jnp.maximum(s - 1, 0)))

        def value_pass(s, carry):
            total, out = carry
            weights = jnp.exp2((store[s] - top) * (SCALE * LOG2E))
            store[s] = weights
            out = out + tn(kv(1, stored_at(s)), weights.astype(BF))
            return total + fold(jnp.add, weights), out

        total, out = lax.fori_loop(
            0, n, value_pass, (jnp.zeros((8, ROWS), F32), jnp.zeros((HD, ROWS), F32))
        )
        norm = 1.0 / jnp.sum(total, axis=0, keepdims=True)
        out_low = jnp.transpose(out * norm).astype(BF)
        delta = jnp.sum(
            jnp.transpose(g.astype(F32) * out_low.astype(F32)), axis=0, keepdims=True
        )
        for h in range(HEADS):
            out_ref[at, h * HD : (h + 1) * HD] = out_low[h * BLK : (h + 1) * BLK]

        def grad_pass(s, dq):
            j = stored_at(s)
            k_tile, v_tile = kv(0, j), kv(1, j)
            weights = store[s] * norm
            acc[1, j] += nn(weights.astype(BF), g)
            grad = (weights * (nt(v_tile, g) - delta)).astype(BF)
            acc[0, j] += nn(grad, q)
            return dq + tn(k_tile, grad)

        dq = lax.fori_loop(0, n, grad_pass, jnp.zeros((HD, ROWS), F32))
        dq = jnp.transpose(dq * SCALE).astype(BF)
        for h in range(HEADS):
            dq_ref[at, h * HD : (h + 1) * HD] = dq[h * BLK : (h + 1) * BLK]
        return carry

    lax.fori_loop(0, 2, own_block, 0)
    own_scale = jnp.where(core == 0, SCALE, 1.0)
    other_scale = jnp.where(core == 0, 1.0, SCALE)
    for r in range(8):
        for part in range(2):
            target = 2 * ((x if part == 0 else 1 - x) * 8 + lax.rem(z + r, 8))
            for half in range(2):
                rows = pl.ds((2 * part + half) * BLK, BLK)
                mine_ref[r, rows, :] = (acc[core, target + half] * own_scale).astype(BF)
                other_ref[r, rows, :] = (acc[1 - core, target + half] * other_scale).astype(BF)


def attention(ids, vis, count, order, query, grad_out, segments, pieces):
    smem = pl.BlockSpec(memory_space=pltpu.SMEM)
    vmem = pl.BlockSpec(memory_space=pltpu.VMEM)
    anywhere = pl.BlockSpec(memory_space=pl.ANY)
    part = jax.ShapeDtypeStruct((8, 4 * BLK, HD), BF)
    return pl.pallas_call(
        attention_kernel,
        in_specs=[smem] * 4 + [vmem] * 3 + [anywhere] * len(pieces),
        out_specs=[vmem] * 4,
        out_shape=[
            jax.ShapeDtypeStruct(query.shape, BF),
            jax.ShapeDtypeStruct(query.shape, BF),
            part,
            part,
        ],
        scratch_shapes=[
            pltpu.VMEM((2, 16, 2 * BLK, HD), BF),
            pltpu.VMEM((24, BLK, ROWS), F32),
            pltpu.VMEM((2, NB, BLK, HD), F32),
            pltpu.SMEM((NB,), jnp.int32),
            pltpu.SemaphoreType.DMA((2 * len(pieces),)),
        ],
        compiler_params=pltpu.CompilerParams(vmem_limit_bytes=48 * 1024 * 1024),
        name="attention",
    )(ids, vis, count, order, query, grad_out, segments, *pieces)


def assemble_kernel(ids, *rest):
    pieces, out_ref = rest[:-1], rest[-1]
    xh, y, core = ids[2], ids[3], ids[4]
    shifts = (0,) + Y_SHIFTS
    n_piece = len(shifts)
    for p, piece in enumerate(pieces):
        which = core if p < n_piece else 1 - core
        source_y = lax.rem(y - shifts[p % n_piece] + 4, 4)
        for part in range(2):
            source_xh = xh if part == 0 else 1 - xh
            column = (2 * (source_xh * 4 + source_y) + which) * HD
            out_ref[:, pl.ds(pl.multiple_of(column, HD), HD)] = piece[
                part * 2 * BLK : (part + 1) * 2 * BLK, :
            ].astype(F32)


def assemble(ids, pieces):
    smem = pl.BlockSpec(memory_space=pltpu.SMEM)
    vmem = pl.BlockSpec(memory_space=pltpu.VMEM)
    return pl.pallas_call(
        assemble_kernel,
        in_specs=[smem] + [vmem] * len(pieces),
        out_specs=vmem,
        out_shape=jax.ShapeDtypeStruct((2 * BLK, 2 * KVH * HD), F32),
        compiler_params=pltpu.CompilerParams(vmem_limit_bytes=32 * 1024 * 1024),
        name="assemble",
    )(ids, *pieces)


def shards(query, keyval, grad_out, vis_blocks, vis_count, segment_ids, block_order):
    x, z, xh, y, core = (lax.axis_index(a) for a in ("x", "z", "xh", "y", "core"))
    ids = jnp.stack([x, z, xh, y, core]).astype(jnp.int32)
    mine = lax.dynamic_slice_in_dim(keyval, ((xh * 4 + y) * 2 + core) * HD, HD, 1)
    both = jnp.concatenate([mine, swap(mine, "x")], axis=0)
    pieces = [both] + [shift(both, "z", 8, k) for k in Z_SHIFTS]
    pieces = pieces + [swap(p, "core") for p in pieces]
    attn_out, grad_query, mine, other = attention(
        ids, vis_blocks, vis_count, block_order, query, grad_out, segment_ids.reshape(NB, BLK), pieces
    )
    got = swap(other, "core")
    joined = (mine.astype(F32) + got.astype(F32)).astype(BF)
    got = [shift(joined[k % 8], "z", 8, k) for k in Z_SHIFTS]
    summed = functools.reduce(jnp.add, [g.astype(F32) for g in got], joined[0].astype(F32)).astype(BF)
    got = swap(summed[2 * BLK :], "x")
    summed = (summed[: 2 * BLK].astype(F32) + got.astype(F32)).astype(BF)
    both = jnp.concatenate([summed, swap(summed, "xh")], axis=0)
    pieces = [both] + [shift(both, "y", 4, k) for k in Y_SHIFTS]
    pieces = pieces + [swap(p, "core") for p in pieces]
    return attn_out, grad_query, assemble(ids, pieces)


def solution(mesh):
    fine = Mesh(mesh.devices.reshape(2, 8, 2, 4, 2), ("x", "z", "xh", "y", "core"))
    ctx, head = ("x", "z"), ("xh", "y", "core")
    return jax.shard_map(
        shards,
        mesh=fine,
        in_specs=(P(ctx, head), P(ctx, None), P(ctx, head), P(), P(), P(), P()),
        out_specs=(P(ctx, head), P(ctx, head), P(ctx, None)),
        check_vma=False,
    )
```

```python
import functools

import jax
import jax.numpy as jnp
from jax import lax
from jax.experimental import pallas as pl
from jax.experimental.pallas import tpu as pltpu
from jax.sharding import Mesh, PartitionSpec as P

QH = 64
KVH = 8
HD = 128
BLK = 128
NB = 32
HEADS = 4
GROUP = 4
ROWS = HEADS * BLK
SCALE = HD**-0.5
LOG2E = 1.4426950408889634
MASKED = -1e30
BF = jnp.bfloat16
F32 = jnp.float32


def shift(value, axis, size, by):
    return lax.ppermute(value, axis, [(i, (i + by) % size) for i in range(size)])


def swap(value, axis):
    return lax.ppermute(value, axis, [(0, 1), (1, 0)])


def nt(a, b):
    return lax.dot_general(a, b, (((1,), (1,)), ((), ())), preferred_element_type=F32)


def nn(a, b):
    return lax.dot_general(a, b, (((1,), (0,)), ((), ())), preferred_element_type=F32)


def tn(a, b):
    return lax.dot_general(a, b, (((0,), (0,)), ((), ())), preferred_element_type=F32)


def attention_kernel(
    vis_any, count_any, order_any, q_any, g_any, seg_any, k_ref, v_ref,
    out_any, dq_any, mine_ref, other_ref,
    store, low, diag_scr, low_diag, accum, q_scr, g_scr, acc, q_ref, g_ref, seg_ref, out_ref, dq_ref,
    vis, count, order, inv, io_sem,
):
    x, z, core = lax.axis_index("x"), lax.axis_index("z"), lax.axis_index("core")
    own = x * 8 + z
    pairs = [
        (order_any, order),
        (count_any, count),
        (vis_any, vis),
        (q_any, q_ref),
        (seg_any, seg_ref),
        (g_any, g_ref),
    ]
    inputs = [pltpu.make_async_copy(*pair, io_sem.at[k]) for k, pair in enumerate(pairs)]
    for copy in inputs:
        copy.start()
    acc[...] = jnp.zeros_like(acc)
    inputs[0].wait()

    def place(j, carry):
        shard = j // 2
        by_z = lax.rem(shard - z + 16, 8)
        by_x = jnp.where(shard // 8 == x, 0, 2)
        inv[order[j]] = 4 * by_z + by_x + lax.rem(j, 2)
        return carry

    lax.fori_loop(0, NB, place, 0)
    for copy in inputs[1:5]:
        copy.wait()

    u_pos = lax.broadcasted_iota(jnp.int32, (BLK, BLK), 0)
    t_pos = lax.broadcasted_iota(jnp.int32, (BLK, BLK), 1)

    def kv(which, j):
        return (k_ref, v_ref)[which][pl.ds(pl.multiple_of(j * BLK, BLK), BLK), :]

    def listed(b, n, s):
        s = jnp.minimum(s, n - 1)
        v = vis[b, s]
        return inv[jnp.where(v < b, v, vis[b, s + 1])]

    def fold(fn, value):
        return functools.reduce(fn, [value[8 * r : 8 * r + 8] for r in range(value.shape[0] // 8)])

    blocks = [order[2 * own + i] for i in range(2)]
    counts = [count[b] - 1 for b in blocks]
    groups = [(n + GROUP - 1) // GROUP for n in counts]
    diags = [0, 1]
    tops, totals, deltas = [], [], []

    def tiles(i, group, which):
        stored = [listed(blocks[i], counts[i], group * GROUP + r) for r in range(GROUP)]
        return stored, jnp.concatenate([kv(which, j) for j in stored], axis=0)

    for i in range(2):
        at = slice(i * BLK, (i + 1) * BLK)
        for h in range(HEADS):
            q_scr[i, h * BLK : (h + 1) * BLK, :] = q_ref[at, h * HD : (h + 1) * HD]
        seg_t = jnp.broadcast_to(seg_ref[pl.ds(blocks[i], 1), :], (BLK, BLK))
        seg_u = jnp.transpose(seg_t)
        seen = (u_pos <= t_pos) & (seg_u == seg_t)
        seen = jnp.concatenate([seen.astype(F32)] * HEADS, axis=1) > 0.5
        scores = jnp.where(seen, nt(kv(0, diags[i]), q_scr[i]), MASKED)
        diag_scr[i] = scores
        tops.append(fold(jnp.maximum, scores))

    for i in range(2):

        def score_pass(group, top, i=i):
            _, keys = tiles(i, group, 0)
            scores = nt(keys, q_scr[i])
            store[i, group] = scores
            return jnp.maximum(top, fold(jnp.maximum, scores))

        tops[i] = lax.fori_loop(0, groups[i], score_pass, tops[i])

    for i in range(2):
        tops[i] = jnp.max(tops[i], axis=0, keepdims=True)
        weights = jnp.exp2((diag_scr[i] - tops[i]) * (SCALE * LOG2E))
        totals.append(fold(jnp.add, weights))
        weights = weights.astype(BF)
        low_diag[i] = weights
        accum[i] = tn(kv(1, diags[i]), weights)

    for i in range(2):

        def value_pass(group, total, i=i):
            lows = []
            for r in range(GROUP):
                base = jnp.where(group * GROUP + r < counts[i], tops[i], -MASKED)
                weights = jnp.exp2((store[i, group, r * BLK : (r + 1) * BLK] - base) * (SCALE * LOG2E))
                total = total + fold(jnp.add, weights)
                lows.append(weights.astype(BF))
            lows = jnp.concatenate(lows, axis=0)
            low[i, group] = lows
            _, values = tiles(i, group, 1)
            accum[i] += tn(values, lows)
            return total

        totals[i] = lax.fori_loop(0, groups[i], value_pass, totals[i])

    def grads(i, weights, values, stored):
        g = g_scr[i]
        grad = (weights.astype(F32) * (nt(values, g) - deltas[i])).astype(BF)
        grad_values = nn(weights, g)
        grad_keys = nn(grad, q_scr[i])
        for r, j in enumerate(stored):
            acc[1, j] += grad_values[r * BLK : (r + 1) * BLK]
            acc[0, j] += grad_keys[r * BLK : (r + 1) * BLK]
        return grad

    inputs[5].wait()
    eighth = jnp.full((16, HD), 0.125, BF)
    ones = jnp.ones((8, HD), BF)
    for i in range(2):
        at = slice(i * BLK, (i + 1) * BLK)
        norm = 1.0 / jnp.sum(totals[i], axis=0, keepdims=True)
        out_low = jnp.transpose((accum[i] * norm).astype(BF))
        norm = jnp.broadcast_to(norm, (8, ROWS))
        high = norm.astype(BF)
        rest_low = (norm - high.astype(F32)).astype(BF)
        norm_col = tn(jnp.concatenate([high, rest_low], axis=0), eighth)
        delta = jnp.zeros((8, ROWS), F32)
        for h in range(HEADS):
            rows = slice(h * BLK, (h + 1) * BLK)
            out_ref[at, h * HD : (h + 1) * HD] = out_low[rows]
            g = g_ref[at, h * HD : (h + 1) * HD].astype(F32)
            g_scr[i, rows, :] = (g * norm_col[rows]).astype(BF)
        g = g_scr[i].astype(F32) * out_low.astype(F32)
        high = g.astype(BF)
        rest_low = (g - high.astype(F32)).astype(BF)
        deltas.append((nt(ones, high) + nt(ones, rest_low))[0:1])
    outputs = [
        pltpu.make_async_copy(out_ref, out_any, io_sem.at[6]),
        pltpu.make_async_copy(dq_ref, dq_any, io_sem.at[7]),
    ]
    outputs[0].start()
    for i in range(2):
        accum[i] = tn(kv(0, diags[i]), grads(i, low_diag[i], kv(1, diags[i]), diags[i : i + 1]))

    for i in range(2):

        def grad_pass(group, carry, i=i):
            stored, values = tiles(i, group, 1)
            _, keys = tiles(i, group, 0)
            accum[i] += tn(keys, grads(i, low[i, group], values, stored))
            return carry

        lax.fori_loop(0, groups[i], grad_pass, 0)

    for i in range(2):
        at = slice(i * BLK, (i + 1) * BLK)
        dq = jnp.transpose((accum[i] * SCALE).astype(BF))
        for h in range(HEADS):
            dq_ref[at, h * HD : (h + 1) * HD] = dq[h * BLK : (h + 1) * BLK]

    outputs[1].start()
    own_scale = jnp.where(core == 0, SCALE, 1.0)
    other_scale = jnp.where(core == 0, 1.0, SCALE)
    for r in range(8):
        at = slice(4 * r, 4 * r + 4)
        mine_ref[r] = (acc[core, at] * own_scale).astype(BF).reshape(4 * BLK, HD)
        other_ref[r] = (acc[1 - core, at] * other_scale).astype(BF).reshape(4 * BLK, HD)
    for copy in outputs:
        copy.wait()


def attention(vis, count, order, query, grad_out, segments, keys, values):
    vmem = pl.BlockSpec(memory_space=pltpu.VMEM)
    hbm = pl.BlockSpec(memory_space=pltpu.HBM)
    part = jax.ShapeDtypeStruct((8, 4 * BLK, HD), BF)
    return pl.pallas_call(
        attention_kernel,
        in_specs=[hbm] * 6 + [vmem] * 2,
        out_specs=[hbm] * 2 + [vmem] * 2,
        out_shape=[
            jax.ShapeDtypeStruct(query.shape, BF),
            jax.ShapeDtypeStruct(query.shape, BF),
            part,
            part,
        ],
        scratch_shapes=[
            pltpu.VMEM((2, 24 // GROUP, GROUP * BLK, ROWS), F32),
            pltpu.VMEM((2, 24 // GROUP, GROUP * BLK, ROWS), BF),
            pltpu.VMEM((2, BLK, ROWS), F32),
            pltpu.VMEM((2, BLK, ROWS), BF),
            pltpu.VMEM((2, HD, ROWS), F32),
            pltpu.VMEM((2, ROWS, HD), BF),
            pltpu.VMEM((2, ROWS, HD), BF),
            pltpu.VMEM((2, NB, BLK, HD), F32),
            pltpu.VMEM(query.shape, BF),
            pltpu.VMEM(query.shape, BF),
            pltpu.VMEM((NB, BLK), jnp.int32),
            pltpu.VMEM(query.shape, BF),
            pltpu.VMEM(query.shape, BF),
            pltpu.SMEM(vis.shape, jnp.int32),
            pltpu.SMEM((NB,), jnp.int32),
            pltpu.SMEM((NB,), jnp.int32),
            pltpu.SMEM((NB,), jnp.int32),
            pltpu.SemaphoreType.DMA((8,)),
        ],
        compiler_params=pltpu.CompilerParams(vmem_limit_bytes=48 * 1024 * 1024),
        name="attention",
    )(vis, count, order, query, grad_out, segments, keys, values)


def assemble_kernel(mine_ref, other_ref, out_ref):
    core = lax.axis_index("core")
    for y in range(4):
        for xh in range(2):
            rows = slice((2 * y + xh) * 2 * BLK, (2 * y + xh + 1) * 2 * BLK)
            for ref, which in ((mine_ref, core), (other_ref, 1 - core)):
                column = pl.multiple_of((2 * (xh * 4 + y) + which) * HD, HD)
                out_ref[:, pl.ds(column, HD)] = ref[rows, :].astype(F32)


def assemble(mine, other):
    vmem = pl.BlockSpec(memory_space=pltpu.VMEM)
    return pl.pallas_call(
        assemble_kernel,
        in_specs=[vmem] * 2,
        out_specs=vmem,
        out_shape=jax.ShapeDtypeStruct((2 * BLK, 2 * KVH * HD), F32),
        compiler_params=pltpu.CompilerParams(vmem_limit_bytes=32 * 1024 * 1024),
        name="assemble",
    )(mine, other)


def wide(*parts):
    return functools.reduce(jnp.add, [p.astype(F32) for p in parts])


def shards(query, keyval, grad_out, vis_blocks, vis_count, segment_ids, block_order):
    xh, y, core = (lax.axis_index(a) for a in ("xh", "y", "core"))
    half = 2 * BLK
    mine = lax.dynamic_slice_in_dim(keyval, ((xh * 4 + y) * 2 + core) * HD, HD, 1)
    both = jnp.concatenate([mine, swap(mine, "x")], axis=0)
    up2, down2 = shift(both, "z", 8, 2), shift(both, "z", 8, -2)
    up1, down1 = shift(both, "z", 8, 1), shift(both, "z", 8, -1)
    up4, down4 = shift(up2[:half], "z", 8, 2), shift(down2[half:], "z", 8, -2)
    up3, down3 = shift(up2, "z", 8, 1), shift(down2, "z", 8, -1)
    mine = jnp.concatenate([both, down1, down2, down3, up4, down4, up3, up2, up1], axis=0)
    other = swap(mine, "core")
    keys, values = jnp.where(core == 0, mine, other), jnp.where(core == 0, other, mine)
    attn_out, grad_query, mine, other = attention(
        vis_blocks, vis_count, block_order, query, grad_out, segment_ids.reshape(NB, BLK), keys, values
    )
    joined = wide(mine, swap(other, "core")).astype(BF)
    for4_up, for4_down = shift(joined[4, :half], "z", 8, 2), shift(joined[4, half:], "z", 8, -2)
    for3_up, for3_down = shift(joined[3], "z", 8, 1), shift(joined[5], "z", 8, -1)
    up2 = jnp.concatenate(
        [wide(joined[2, :half], for3_up[:half], for4_up), wide(joined[2, half:], for3_up[half:])], axis=0
    )
    down2 = jnp.concatenate(
        [wide(joined[6, :half], for3_down[:half]), wide(joined[6, half:], for3_down[half:], for4_down)], axis=0
    )
    for2_up, for2_down = shift(up2.astype(BF), "z", 8, 2), shift(down2.astype(BF), "z", 8, -2)
    near_up, near_down, _ = lax.optimization_barrier((joined[1], joined[7], for3_down))
    for1_up, for1_down = shift(near_up, "z", 8, 1), shift(near_down, "z", 8, -1)
    summed = wide(joined[0], for1_up, for1_down, for2_up, for2_down)
    got = swap(summed[half:].astype(BF), "x")
    summed = wide(summed[:half], got).astype(BF)
    mine = lax.all_to_all(jnp.concatenate([summed] * KVH, axis=0), ("y", "xh"), 0, 0, tiled=True)
    return attn_out, grad_query, assemble(mine, swap(mine, "core"))


def solution(mesh):
    fine = Mesh(mesh.devices.reshape(2, 8, 2, 4, 2), ("x", "z", "xh", "y", "core"))
    ctx, head = ("x", "z"), ("xh", "y", "core")
    return jax.shard_map(
        shards,
        mesh=fine,
        in_specs=(P(ctx, head), P(ctx, None), P(ctx, head), P(), P(), P(), P()),
        out_specs=(P(ctx, head), P(ctx, head), P(ctx, None)),
        check_vma=False,
    )
```

```python
import functools

import jax
import jax.numpy as jnp
from jax import lax
from jax.experimental import pallas as pl
from jax.experimental.pallas import tpu as pltpu
from jax.sharding import Mesh, PartitionSpec as P

QH = 64
KVH = 8
HD = 128
BLK = 128
NB = 32
HEADS = 4
GROUP = 4
REACHED = (0, 1, 2, 6, 7)
RELAYED = (3, 4, 5)
ROWS = HEADS * BLK
SCALE = HD**-0.5
LOG2E = 1.4426950408889634
MASKED = -1e30
BF = jnp.bfloat16
F32 = jnp.float32


def shift(value, axis, size, by):
    return lax.ppermute(value, axis, [(i, (i + by) % size) for i in range(size)])


def swap(value, axis):
    return lax.ppermute(value, axis, [(0, 1), (1, 0)])


def nt(a, b):
    return lax.dot_general(a, b, (((1,), (1,)), ((), ())), preferred_element_type=F32)


def nn(a, b):
    return lax.dot_general(a, b, (((1,), (0,)), ((), ())), preferred_element_type=F32)


def tn(a, b):
    return lax.dot_general(a, b, (((0,), (0,)), ((), ())), preferred_element_type=F32)


def attention_kernel(
    vis_any, count_any, order_any, q_any, g_any, seg_any, kv_ref,
    out_any, dq_any, other_relayed_ref, mine_relayed_ref, other_ref, mine_ref,
    store, low, accum, q_scr, g_scr, acc, q_ref, g_ref, seg_ref, out_ref, dq_ref,
    vis, count, order, inv, io_sem,
):
    x, z, core = lax.axis_index("x"), lax.axis_index("z"), lax.axis_index("core")
    own = x * 8 + z
    pairs = [
        (order_any, order),
        (count_any, count),
        (vis_any, vis),
        (q_any, q_ref),
        (seg_any, seg_ref),
        (g_any, g_ref),
    ]
    inputs = [pltpu.make_async_copy(*pair, io_sem.at[k]) for k, pair in enumerate(pairs)]
    for copy in inputs:
        copy.start()
    acc[...] = jnp.zeros_like(acc)
    inputs[0].wait()

    def place(j, carry):
        shard = j // 2
        by_z = lax.rem(shard - z + 16, 8)
        at = jnp.where(by_z < 3, by_z, jnp.where(by_z > 5, by_z - 3, by_z + 2))
        inv[order[j]] = jnp.where(shard // 8 == x, 0, 16) + 2 * at + lax.rem(j, 2)
        return carry

    lax.fori_loop(0, NB, place, 0)
    for copy in inputs[1:5]:
        copy.wait()

    u_pos = lax.broadcasted_iota(jnp.int32, (BLK, BLK), 0)
    t_pos = lax.broadcasted_iota(jnp.int32, (BLK, BLK), 1)

    def kv(which, j):
        return kv_ref[pl.ds(pl.multiple_of(j * BLK, BLK), BLK), which * HD : (which + 1) * HD]

    def listed(i, s):
        s = jnp.minimum(s, counts[i] - 1)
        b = blocks[i]
        v = vis[b, jnp.maximum(s - 1, 0)]
        return jnp.where(s == 0, i, inv[jnp.where(v < b, v, vis[b, s])])

    def fold(fn, value):
        return functools.reduce(fn, [value[8 * r : 8 * r + 8] for r in range(value.shape[0] // 8)])

    blocks = [order[2 * own + i] for i in range(2)]
    counts = [count[b] for b in blocks]
    groups = [(n + GROUP - 1) // GROUP for n in counts]
    tops, totals, deltas = [], [], []

    def tiles(i, group, which):
        stored = [listed(i, group * GROUP + r) for r in range(GROUP)]
        return stored, jnp.concatenate([kv(which, j) for j in stored], axis=0)

    for i in range(2):
        at = slice(i * BLK, (i + 1) * BLK)
        for h in range(HEADS):
            q_scr[i, h * BLK : (h + 1) * BLK, :] = q_ref[at, h * HD : (h + 1) * HD]
        seg_t = jnp.broadcast_to(seg_ref[pl.ds(blocks[i], 1), :], (BLK, BLK))
        seg_u = jnp.transpose(seg_t)
        seen = (u_pos <= t_pos) & (seg_u == seg_t)
        seen = jnp.concatenate([seen.astype(F32)] * HEADS, axis=1) > 0.5
        _, keys = tiles(i, 0, 0)
        scores = nt(keys, q_scr[i])
        for r in range(GROUP):
            ok = seen if r == 0 else counts[i] > r
            part = jnp.where(ok, scores[r * BLK : (r + 1) * BLK], MASKED)
            store[i, 0, r * BLK : (r + 1) * BLK] = part
            top = fold(jnp.maximum, part) if r == 0 else jnp.maximum(top, fold(jnp.maximum, part))
        tops.append(top)
        totals.append(jnp.zeros((8, ROWS), F32))
        accum[i] = jnp.zeros((HD, ROWS), F32)

    for i in range(2):

        def score_pass(group, top, i=i):
            _, keys = tiles(i, group, 0)
            scores = nt(keys, q_scr[i])
            store[i, group] = scores
            return jnp.maximum(top, fold(jnp.maximum, scores))

        tops[i] = lax.fori_loop(1, groups[i], score_pass, tops[i])

    for i in range(2):
        tops[i] = jnp.max(tops[i], axis=0, keepdims=True)

    for i in range(2):

        def value_pass(group, total, i=i):
            lows = []
            for r in range(GROUP):
                base = jnp.where(group * GROUP + r < counts[i], tops[i], -MASKED)
                weights = jnp.exp2((store[i, group, r * BLK : (r + 1) * BLK] - base) * (SCALE * LOG2E))
                total = total + fold(jnp.add, weights)
                lows.append(weights.astype(BF))
            lows = jnp.concatenate(lows, axis=0)
            low[i, group] = lows
            _, values = tiles(i, group, 1)
            accum[i] += tn(values, lows)
            return total

        totals[i] = lax.fori_loop(0, groups[i], value_pass, totals[i])

    def grads(i, weights, values, stored):
        g = g_scr[i]
        grad = (weights.astype(F32) * (nt(values, g) - deltas[i])).astype(BF)
        grad_values = nn(weights, g)
        grad_keys = nn(grad, q_scr[i])
        for r, j in enumerate(stored):
            acc[1, j] += grad_values[r * BLK : (r + 1) * BLK]
            acc[0, j] += grad_keys[r * BLK : (r + 1) * BLK]
        return grad

    inputs[5].wait()
    eighth = jnp.full((16, HD), 0.125, BF)
    ones = jnp.ones((8, HD), BF)
    for i in range(2):
        at = slice(i * BLK, (i + 1) * BLK)
        norm = 1.0 / jnp.sum(totals[i], axis=0, keepdims=True)
        out_low = jnp.transpose((accum[i] * norm).astype(BF))
        norm = jnp.broadcast_to(norm, (8, ROWS))
        high = norm.astype(BF)
        rest_low = (norm - high.astype(F32)).astype(BF)
        norm_col = tn(jnp.concatenate([high, rest_low], axis=0), eighth)
        delta = jnp.zeros((8, ROWS), F32)
        for h in range(HEADS):
            rows = slice(h * BLK, (h + 1) * BLK)
            out_ref[at, h * HD : (h + 1) * HD] = out_low[rows]
            g = g_ref[at, h * HD : (h + 1) * HD].astype(F32)
            g_scr[i, rows, :] = (g * norm_col[rows]).astype(BF)
        g = g_scr[i].astype(F32) * out_low.astype(F32)
        high = g.astype(BF)
        rest_low = (g - high.astype(F32)).astype(BF)
        deltas.append((nt(ones, high) + nt(ones, rest_low))[0:1])
    outputs = [
        pltpu.make_async_copy(out_ref, out_any, io_sem.at[6]),
        pltpu.make_async_copy(dq_ref, dq_any, io_sem.at[7]),
    ]
    outputs[0].start()
    for i in range(2):
        accum[i] = jnp.zeros((HD, ROWS), F32)

    for i in range(2):

        def grad_pass(group, carry, i=i):
            stored, values = tiles(i, group, 1)
            _, keys = tiles(i, group, 0)
            accum[i] += tn(keys, grads(i, low[i, group], values, stored))
            return carry

        lax.fori_loop(0, groups[i], grad_pass, 0)

    for i in range(2):
        at = slice(i * BLK, (i + 1) * BLK)
        dq = jnp.transpose((accum[i] * SCALE).astype(BF))
        for h in range(HEADS):
            dq_ref[at, h * HD : (h + 1) * HD] = dq[h * BLK : (h + 1) * BLK]

    outputs[1].start()
    for ref, side, start in (
        (other_relayed_ref, 1 - core, 5),
        (mine_relayed_ref, core, 5),
        (other_ref, 1 - core, 0),
        (mine_ref, core, 0),
    ):
        for r in range(ref.shape[0]):
            at = pl.ds(16 * side + 2 * (start + r), 2)
            ref[r, :, :HD] = (acc[0, at] * SCALE).astype(BF).reshape(2 * BLK, HD)
            ref[r, :, HD:] = acc[1, at].astype(BF).reshape(2 * BLK, HD)
    for copy in outputs:
        copy.wait()


def attention(vis, count, order, query, grad_out, segments, gathered):
    vmem = pl.BlockSpec(memory_space=pltpu.VMEM)
    hbm = pl.BlockSpec(memory_space=pltpu.HBM)
    parts = [jax.ShapeDtypeStruct((n, 2 * BLK, 2 * HD), BF) for n in (len(RELAYED), len(REACHED)) for _ in range(2)]
    return pl.pallas_call(
        attention_kernel,
        in_specs=[hbm] * 6 + [vmem],
        out_specs=[hbm] * 2 + [vmem] * 4,
        out_shape=[
            jax.ShapeDtypeStruct(query.shape, BF),
            jax.ShapeDtypeStruct(query.shape, BF),
            *parts,
        ],
        scratch_shapes=[
            pltpu.VMEM((2, 24 // GROUP, GROUP * BLK, ROWS), F32),
            pltpu.VMEM((2, 24 // GROUP, GROUP * BLK, ROWS), BF),
            pltpu.VMEM((2, HD, ROWS), F32),
            pltpu.VMEM((2, ROWS, HD), BF),
            pltpu.VMEM((2, ROWS, HD), BF),
            pltpu.VMEM((2, NB, BLK, HD), F32),
            pltpu.VMEM(query.shape, BF),
            pltpu.VMEM(query.shape, BF),
            pltpu.VMEM((NB, BLK), jnp.int32),
            pltpu.VMEM(query.shape, BF),
            pltpu.VMEM(query.shape, BF),
            pltpu.SMEM(vis.shape, jnp.int32),
            pltpu.SMEM((NB,), jnp.int32),
            pltpu.SMEM((NB,), jnp.int32),
            pltpu.SMEM((NB,), jnp.int32),
            pltpu.SemaphoreType.DMA((8,)),
        ],
        compiler_params=pltpu.CompilerParams(vmem_limit_bytes=48 * 1024 * 1024),
        name="attention",
    )(vis, count, order, query, grad_out, segments, gathered)


def assemble_kernel(mine_ref, other_ref, out_ref):
    core = lax.axis_index("core")
    for y in range(4):
        for xh in range(2):
            rows = slice((2 * y + xh) * 2 * BLK, (2 * y + xh + 1) * 2 * BLK)
            for ref, which in ((mine_ref, core), (other_ref, 1 - core)):
                column = pl.multiple_of((2 * (xh * 4 + y) + which) * HD, HD)
                out_ref[:, pl.ds(column, HD)] = ref[rows, :].astype(F32)


def assemble(mine, other):
    vmem = pl.BlockSpec(memory_space=pltpu.VMEM)
    return pl.pallas_call(
        assemble_kernel,
        in_specs=[vmem] * 2,
        out_specs=vmem,
        out_shape=jax.ShapeDtypeStruct((2 * BLK, 2 * KVH * HD), F32),
        compiler_params=pltpu.CompilerParams(vmem_limit_bytes=32 * 1024 * 1024),
        name="assemble",
    )(mine, other)


def wide(*parts):
    return functools.reduce(jnp.add, [p.astype(F32) for p in parts])


def shards(query, keyval, grad_out, vis_blocks, vis_count, segment_ids, block_order):
    xh, y, core = (lax.axis_index(a) for a in ("xh", "y", "core"))
    first = core == 0

    def across(value, by):
        pairs = [
            ((a * 8 + i) * 2 + c, ((a ^ c) * 8 + (i + by) % 8) * 2 + c)
            for a in range(2)
            for i in range(8)
            for c in range(2)
            if by or c
        ]
        return lax.ppermute(value, ("x", "z", "core"), pairs)

    def halves(value):
        return jnp.where(first, value[:, :HD], value[:, HD:]), jnp.where(first, value[:, HD:], value[:, :HD])

    near = lax.dynamic_slice_in_dim(keyval, (xh * 4 + y) * 2 * HD, 2 * HD, 1)
    up2, down2 = across(near, 2), across(near, -2)
    up1, down1 = across(near, 1), across(near, -1)
    own = jnp.where(first, near, across(near, 0))
    up3, down3 = shift(up2, "z", 8, 1), shift(down2, "z", 8, -1)
    up4, down4 = shift(up2[:BLK], "z", 8, 2), shift(down2[BLK:], "z", 8, -2)
    reached = jnp.concatenate([own, down1, down2, up2, up1], axis=0)
    relayed = jnp.concatenate([down3, up4, down4, up3], axis=0)
    sides = [(mine, swap(mine, "core")) for mine in (reached, relayed)]
    gathered = [jnp.where(first, mine, other) for mine, other in sides]
    gathered = jnp.concatenate(gathered + [jnp.where(first, other, mine) for mine, other in sides], axis=0)
    attn_out, grad_query, other_relayed, mine_relayed, other, mine = attention(
        vis_blocks, vis_count, block_order, query, grad_out, segment_ids.reshape(NB, BLK), gathered
    )
    relayed = wide(mine_relayed, swap(other_relayed, "core")).astype(BF)
    reached = wide(mine, swap(other, "core")).astype(BF)
    joined = dict(zip(RELAYED + REACHED, [relayed[k] for k in range(3)] + [reached[k] for k in range(5)]))
    for4_up, for4_down = shift(joined[4][:BLK], "z", 8, 2), shift(joined[4][BLK:], "z", 8, -2)
    for3_up, for3_down = shift(joined[3], "z", 8, 1), shift(joined[5], "z", 8, -1)
    up2 = jnp.concatenate(
        [wide(joined[2][:BLK], for3_up[:BLK], for4_up), wide(joined[2][BLK:], for3_up[BLK:])], axis=0
    )
    down2 = jnp.concatenate(
        [wide(joined[6][:BLK], for3_down[:BLK]), wide(joined[6][BLK:], for3_down[BLK:], for4_down)], axis=0
    )
    for2_up, for2_down = across(up2.astype(BF), 2), across(down2.astype(BF), -2)
    for1_up, for1_down = across(joined[1], 1), across(joined[7], -1)
    own = jnp.where(first, joined[0], across(joined[0], 0))
    kept, given = halves(wide(own, for1_up, for1_down, for2_up, for2_down))
    summed = wide(kept, swap(given.astype(BF), "core")).astype(BF)
    mine = lax.all_to_all(jnp.concatenate([summed] * KVH, axis=0), ("y", "xh"), 0, 0, tiled=True)
    return attn_out, grad_query, assemble(mine, swap(mine, "core"))


def solution(mesh):
    fine = Mesh(mesh.devices.reshape(2, 8, 2, 4, 2), ("x", "z", "xh", "y", "core"))
    ctx, head = ("x", "z"), ("xh", "y", "core")
    return jax.shard_map(
        shards,
        mesh=fine,
        in_specs=(P(ctx, head), P(ctx, None), P(ctx, head), P(), P(), P(), P()),
        out_specs=(P(ctx, head), P(ctx, head), P(ctx, None)),
        check_vma=False,
    )
```

```python
import functools

import jax
import jax.numpy as jnp
from jax import lax
from jax.experimental import pallas as pl
from jax.experimental.pallas import tpu as pltpu
from jax.sharding import Mesh, PartitionSpec as P

QH = 64
KVH = 8
HD = 128
BLK = 128
NB = 32
HEADS = 4
GROUP = 4
REACHED = (0, 1, 2, 6, 7)
RELAYED = (3, 4, 5)
ROWS = HEADS * BLK
SCALE = HD**-0.5
LOG2E = 1.4426950408889634
MASKED = -1e30
BF = jnp.bfloat16
F32 = jnp.float32


def shift(value, axis, size, by):
    return lax.ppermute(value, axis, [(i, (i + by) % size) for i in range(size)])


def swap(value, axis):
    return lax.ppermute(value, axis, [(0, 1), (1, 0)])


def nt(a, b):
    return lax.dot_general(a, b, (((1,), (1,)), ((), ())), preferred_element_type=F32)


def nn(a, b):
    return lax.dot_general(a, b, (((1,), (0,)), ((), ())), preferred_element_type=F32)


def tn(a, b):
    return lax.dot_general(a, b, (((0,), (0,)), ((), ())), preferred_element_type=F32)


def attention_kernel(
    vis_any, count_any, order_any, q_any, g_any, seg_any, kv_ref,
    out_any, dq_any, other_relayed_ref, mine_relayed_ref, other_ref, mine_ref,
    store, low, accum, q_scr, g_scr, acc, q_ref, g_ref, seg_ref, out_ref, dq_ref,
    vis, count, order, inv, io_sem,
):
    x, z, core = lax.axis_index("x"), lax.axis_index("z"), lax.axis_index("core")
    own = x * 8 + z
    pairs = [
        (order_any, order),
        (count_any, count),
        (vis_any, vis),
        (q_any, q_ref),
        (seg_any, seg_ref),
        (g_any, g_ref),
    ]
    inputs = [pltpu.make_async_copy(*pair, io_sem.at[k]) for k, pair in enumerate(pairs)]
    for copy in inputs:
        copy.start()
    acc[...] = jnp.zeros_like(acc)
    inputs[0].wait()

    def place(j, carry):
        shard = j // 2
        by_z = lax.rem(shard - z + 16, 8)
        at = jnp.where(by_z < 3, by_z, jnp.where(by_z > 5, by_z - 3, by_z + 2))
        inv[order[j]] = jnp.where(shard // 8 == x, 0, 16) + 2 * at + lax.rem(j, 2)
        return carry

    lax.fori_loop(0, NB, place, 0)
    for copy in inputs[1:5]:
        copy.wait()

    u_pos = lax.broadcasted_iota(jnp.int32, (BLK, BLK), 0)
    t_pos = lax.broadcasted_iota(jnp.int32, (BLK, BLK), 1)

    def kv(which, j):
        return kv_ref[pl.ds(pl.multiple_of(j * BLK, BLK), BLK), which * HD : (which + 1) * HD]

    def listed(i, s):
        s = jnp.minimum(s, counts[i] - 1)
        b = blocks[i]
        v = vis[b, jnp.maximum(s - 1, 0)]
        return jnp.where(s == 0, i, inv[jnp.where(v < b, v, vis[b, s])])

    def fold(fn, value):
        return functools.reduce(fn, [value[8 * r : 8 * r + 8] for r in range(value.shape[0] // 8)])

    blocks = [order[2 * own + i] for i in range(2)]
    counts = [count[b] for b in blocks]
    groups = [(n + GROUP - 1) // GROUP for n in counts]
    tops, totals, deltas = [], [], []

    def tiles(i, group, which):
        stored = [listed(i, group * GROUP + r) for r in range(GROUP)]
        return stored, jnp.concatenate([kv(which, j) for j in stored], axis=0)

    for i in range(2):
        at = slice(i * BLK, (i + 1) * BLK)
        for h in range(HEADS):
            q_scr[i, h * BLK : (h + 1) * BLK, :] = q_ref[at, h * HD : (h + 1) * HD]
        seg_t = jnp.broadcast_to(seg_ref[pl.ds(blocks[i], 1), :], (BLK, BLK))
        seg_u = jnp.transpose(seg_t)
        seen = (u_pos <= t_pos) & (seg_u == seg_t)
        seen = jnp.concatenate([seen.astype(F32)] * HEADS, axis=1) > 0.5
        _, keys = tiles(i, 0, 0)
        scores = nt(keys, q_scr[i])
        for r in range(GROUP):
            ok = seen if r == 0 else counts[i] > r
            part = jnp.where(ok, scores[r * BLK : (r + 1) * BLK], MASKED)
            store[i, 0, r * BLK : (r + 1) * BLK] = part
            top = fold(jnp.maximum, part) if r == 0 else jnp.maximum(top, fold(jnp.maximum, part))
        tops.append(top)
        totals.append(jnp.zeros((8, ROWS), F32))
        accum[i] = jnp.zeros((HD, ROWS), F32)

    for i in range(2):

        def score_pass(group, top, i=i):
            _, keys = tiles(i, group, 0)
            scores = nt(keys, q_scr[i])
            store[i, group] = scores
            return jnp.maximum(top, fold(jnp.maximum, scores))

        tops[i] = lax.fori_loop(1, groups[i], score_pass, tops[i])

    for i in range(2):
        tops[i] = jnp.max(tops[i], axis=0, keepdims=True)

    for i in range(2):

        def value_pass(group, total, i=i):
            lows = []
            for r in range(GROUP):
                base = jnp.where(group * GROUP + r < counts[i], tops[i], -MASKED)
                weights = jnp.exp2((store[i, group, r * BLK : (r + 1) * BLK] - base) * (SCALE * LOG2E))
                total = total + fold(jnp.add, weights)
                lows.append(weights.astype(BF))
            lows = jnp.concatenate(lows, axis=0)
            low[i, group] = lows
            _, values = tiles(i, group, 1)
            accum[i] += tn(values, lows)
            return total

        totals[i] = lax.fori_loop(0, groups[i], value_pass, totals[i])

    def grads(i, weights, values, stored):
        g = g_scr[i]
        grad = (weights.astype(F32) * (nt(values, g) - deltas[i])).astype(BF)
        grad_values = nn(weights, g)
        grad_keys = nn(grad, q_scr[i])
        for r, j in enumerate(stored):
            acc[1, j] += grad_values[r * BLK : (r + 1) * BLK]
            acc[0, j] += grad_keys[r * BLK : (r + 1) * BLK]
        return grad

    inputs[5].wait()
    eighth = jnp.full((16, HD), 0.125, BF)
    ones = jnp.ones((8, HD), BF)
    for i in range(2):
        at = slice(i * BLK, (i + 1) * BLK)
        norm = 1.0 / jnp.sum(totals[i], axis=0, keepdims=True)
        out_low = jnp.transpose((accum[i] * norm).astype(BF))
        norm = jnp.broadcast_to(norm, (8, ROWS))
        high = norm.astype(BF)
        rest_low = (norm - high.astype(F32)).astype(BF)
        norm_col = tn(jnp.concatenate([high, rest_low], axis=0), eighth)
        delta = jnp.zeros((8, ROWS), F32)
        for h in range(HEADS):
            rows = slice(h * BLK, (h + 1) * BLK)
            out_ref[at, h * HD : (h + 1) * HD] = out_low[rows]
            g = g_ref[at, h * HD : (h + 1) * HD].astype(F32)
            g_scr[i, rows, :] = (g * norm_col[rows]).astype(BF)
        g = g_scr[i].astype(F32) * out_low.astype(F32)
        high = g.astype(BF)
        rest_low = (g - high.astype(F32)).astype(BF)
        deltas.append((nt(ones, high) + nt(ones, rest_low))[0:1])
    outputs = [
        pltpu.make_async_copy(out_ref, out_any, io_sem.at[6]),
        pltpu.make_async_copy(dq_ref, dq_any, io_sem.at[7]),
    ]
    outputs[0].start()
    for i in range(2):
        accum[i] = jnp.zeros((HD, ROWS), F32)

    for i in range(2):

        def grad_pass(group, carry, i=i):
            stored, values = tiles(i, group, 1)
            _, keys = tiles(i, group, 0)
            accum[i] += tn(keys, grads(i, low[i, group], values, stored))
            return carry

        lax.fori_loop(0, groups[i], grad_pass, 0)

    for i in range(2):
        at = slice(i * BLK, (i + 1) * BLK)
        dq = jnp.transpose((accum[i] * SCALE).astype(BF))
        for h in range(HEADS):
            dq_ref[at, h * HD : (h + 1) * HD] = dq[h * BLK : (h + 1) * BLK]

    outputs[1].start()
    for ref, side, start in (
        (other_relayed_ref, 1 - core, 5),
        (mine_relayed_ref, core, 5),
        (other_ref, 1 - core, 0),
        (mine_ref, core, 0),
    ):
        for r in range(ref.shape[0]):
            at = pl.ds(16 * side + 2 * (start + r), 2)
            ref[r, :, :HD] = (acc[0, at] * SCALE).astype(BF).reshape(2 * BLK, HD)
            ref[r, :, HD:] = acc[1, at].astype(BF).reshape(2 * BLK, HD)
    for copy in outputs:
        copy.wait()


def attention(vis, count, order, query, grad_out, segments, gathered):
    vmem = pl.BlockSpec(memory_space=pltpu.VMEM)
    hbm = pl.BlockSpec(memory_space=pltpu.HBM)
    parts = [jax.ShapeDtypeStruct((n, 2 * BLK, 2 * HD), BF) for n in (len(RELAYED), len(REACHED)) for _ in range(2)]
    return pl.pallas_call(
        attention_kernel,
        in_specs=[hbm] * 6 + [vmem],
        out_specs=[hbm] * 2 + [vmem] * 4,
        out_shape=[
            jax.ShapeDtypeStruct(query.shape, BF),
            jax.ShapeDtypeStruct(query.shape, BF),
            *parts,
        ],
        scratch_shapes=[
            pltpu.VMEM((2, 24 // GROUP, GROUP * BLK, ROWS), F32),
            pltpu.VMEM((2, 24 // GROUP, GROUP * BLK, ROWS), BF),
            pltpu.VMEM((2, HD, ROWS), F32),
            pltpu.VMEM((2, ROWS, HD), BF),
            pltpu.VMEM((2, ROWS, HD), BF),
            pltpu.VMEM((2, NB, BLK, HD), F32),
            pltpu.VMEM(query.shape, BF),
            pltpu.VMEM(query.shape, BF),
            pltpu.VMEM((NB, BLK), jnp.int32),
            pltpu.VMEM(query.shape, BF),
            pltpu.VMEM(query.shape, BF),
            pltpu.SMEM(vis.shape, jnp.int32),
            pltpu.SMEM((NB,), jnp.int32),
            pltpu.SMEM((NB,), jnp.int32),
            pltpu.SMEM((NB,), jnp.int32),
            pltpu.SemaphoreType.DMA((8,)),
        ],
        compiler_params=pltpu.CompilerParams(vmem_limit_bytes=48 * 1024 * 1024),
        name="attention",
    )(vis, count, order, query, grad_out, segments, gathered)


def assemble_kernel(mine_ref, other_ref, out_ref):
    xh, y, core = lax.axis_index("xh"), lax.axis_index("y"), lax.axis_index("core")
    for r, by in enumerate((2, 1, -1, 0)):
        source_y = lax.rem(y - by + 4, 4)
        for ref, side in ((mine_ref, core), (other_ref, 1 - core)):
            source_xh = jnp.where(side == 0, xh, 1 - xh)
            column = pl.multiple_of((source_xh * 4 + source_y) * 2 * HD, 2 * HD)
            out_ref[:, pl.ds(column, 2 * HD)] = ref[r * 2 * BLK : (r + 1) * 2 * BLK, :].astype(F32)


def assemble(mine, other):
    vmem = pl.BlockSpec(memory_space=pltpu.VMEM)
    return pl.pallas_call(
        assemble_kernel,
        in_specs=[vmem] * 2,
        out_specs=vmem,
        out_shape=jax.ShapeDtypeStruct((2 * BLK, 2 * KVH * HD), F32),
        compiler_params=pltpu.CompilerParams(vmem_limit_bytes=32 * 1024 * 1024),
        name="assemble",
    )(mine, other)


def wide(*parts):
    return functools.reduce(jnp.add, [p.astype(F32) for p in parts])


def shards(query, keyval, grad_out, vis_blocks, vis_count, segment_ids, block_order):
    xh, y, core = (lax.axis_index(a) for a in ("xh", "y", "core"))
    first = core == 0

    def across(value, by):
        pairs = [
            ((a * 8 + i) * 2 + c, ((a ^ c) * 8 + (i + by) % 8) * 2 + c)
            for a in range(2)
            for i in range(8)
            for c in range(2)
            if by or c
        ]
        return lax.ppermute(value, ("x", "z", "core"), pairs)

    def split(value, by):
        pairs = [(2 * i + c, 2 * ((i + (by, -by)[c]) % 8) + c) for i in range(8) for c in range(2)]
        return lax.ppermute(value, ("z", "core"), pairs)

    def across_heads(value, by):
        pairs = [
            ((a * 4 + i) * 2 + c, ((a ^ c) * 4 + (i + by) % 4) * 2 + c)
            for a in range(2)
            for i in range(4)
            for c in range(2)
            if by or c
        ]
        return lax.ppermute(value, ("xh", "y", "core"), pairs)

    near = lax.dynamic_slice_in_dim(keyval, (xh * 4 + y) * 2 * HD, 2 * HD, 1)
    up2, down2 = across(near, 2), across(near, -2)
    up1, down1 = across(near, 1), across(near, -1)
    own = jnp.where(first, near, across(near, 0))
    up3, down3 = shift(up2, "z", 8, 1), shift(down2, "z", 8, -1)
    four = split(jnp.where(first, up2, down2), 2)
    reached = jnp.concatenate([own, down1, down2, up2, up1], axis=0)
    relayed = jnp.concatenate([down3, four, up3], axis=0)
    sides = [(mine, swap(mine, "core")) for mine in (reached, relayed)]
    gathered = [jnp.where(first, mine, other) for mine, other in sides]
    gathered = jnp.concatenate(gathered + [jnp.where(first, other, mine) for mine, other in sides], axis=0)
    inputs = (vis_blocks, vis_count, block_order, query, grad_out, segment_ids.reshape(NB, BLK))
    inputs = [pltpu.with_memory_space_constraint(v, pltpu.HBM) for v in inputs]
    attn_out, grad_query, other_relayed, mine_relayed, other, mine = attention(
        *inputs, gathered
    )
    relayed = wide(mine_relayed, swap(other_relayed, "core")).astype(BF)
    reached = wide(mine, swap(other, "core")).astype(BF)
    joined = dict(zip(RELAYED + REACHED, [relayed[k] for k in range(3)] + [reached[k] for k in range(5)]))
    for4 = split(joined[4], 2)
    for3_up, for3_down = shift(joined[3], "z", 8, 1), shift(joined[5], "z", 8, -1)
    zero = jnp.zeros_like(for4)
    up2 = wide(joined[2], for3_up, jnp.where(first, for4, zero))
    down2 = wide(joined[6], for3_down, jnp.where(first, zero, for4))
    for2_up, for2_down = across(up2.astype(BF), 2), across(down2.astype(BF), -2)
    for1_up, for1_down = across(joined[1], 1), across(joined[7], -1)
    own = jnp.where(first, joined[0], across(joined[0], 0))
    summed = wide(own, for1_up, for1_down, for2_up, for2_down).astype(BF)
    summed = wide(summed, swap(summed, "core")).astype(BF)
    pieces = [across_heads(summed, by) for by in (2, 1, -1, 0)]
    pieces[3] = jnp.where(first, summed, pieces[3])
    mine = jnp.concatenate(pieces, axis=0)
    return attn_out, grad_query, assemble(mine, swap(mine, "core"))


def solution(mesh):
    fine = Mesh(mesh.devices.reshape(2, 8, 2, 4, 2), ("x", "z", "xh", "y", "core"))
    ctx, head = ("x", "z"), ("xh", "y", "core")
    return jax.shard_map(
        shards,
        mesh=fine,
        in_specs=(P(ctx, head), P(ctx, None), P(ctx, head), P(), P(), P(), P()),
        out_specs=(P(ctx, head), P(ctx, head), P(ctx, None)),
        check_vma=False,
    )
```

```python
import functools

import jax
import jax.numpy as jnp
from jax import lax
from jax.experimental import pallas as pl
from jax.experimental.pallas import tpu as pltpu
from jax.sharding import Mesh, PartitionSpec as P

QH = 64
KVH = 8
HD = 128
BLK = 128
NB = 32
HEADS = 4
GROUP = 4
REACHED = (0, 1, 2, 6, 7)
RELAYED = (3, 4, 5)
ROWS = HEADS * BLK
SCALE = HD**-0.5
LOG2E = 1.4426950408889634
MASKED = -1e30
BF = jnp.bfloat16
F32 = jnp.float32


def shift(value, axis, size, by):
    return lax.ppermute(value, axis, [(i, (i + by) % size) for i in range(size)])


def swap(value, axis):
    return lax.ppermute(value, axis, [(0, 1), (1, 0)])


def nt(a, b):
    return lax.dot_general(a, b, (((1,), (1,)), ((), ())), preferred_element_type=F32)


def nn(a, b):
    return lax.dot_general(a, b, (((1,), (0,)), ((), ())), preferred_element_type=F32)


def tn(a, b):
    return lax.dot_general(a, b, (((0,), (0,)), ((), ())), preferred_element_type=F32)


def attention_kernel(
    vis_any, count_any, order_any, q_any, g_any, seg_any, kv_ref,
    out_any, dq_any, other_relayed_ref, mine_relayed_ref, other_ref, mine_ref,
    store, low, accum, q_scr, g_scr, acc, q_ref, g_ref, seg_ref, out_ref, dq_ref,
    vis, count, order, inv, io_sem,
):
    x, z, core = lax.axis_index("x"), lax.axis_index("z"), lax.axis_index("core")
    own = x * 8 + z
    pairs = [
        (order_any, order),
        (count_any, count),
        (vis_any, vis),
        (q_any, q_ref),
        (seg_any, seg_ref),
        (g_any, g_ref),
    ]
    inputs = [pltpu.make_async_copy(*pair, io_sem.at[k]) for k, pair in enumerate(pairs)]
    for copy in inputs:
        copy.start()
    acc[...] = jnp.zeros_like(acc)
    inputs[0].wait()

    def place(j, carry):
        shard = j // 2
        by_z = lax.rem(shard - z + 16, 8)
        at = jnp.where(by_z < 3, by_z, jnp.where(by_z > 5, by_z - 3, by_z + 2))
        inv[order[j]] = jnp.where(shard // 8 == x, 0, 16) + 2 * at + lax.rem(j, 2)
        return carry

    lax.fori_loop(0, NB, place, 0)
    for copy in inputs[1:5]:
        copy.wait()

    u_pos = lax.broadcasted_iota(jnp.int32, (BLK, BLK), 0)
    t_pos = lax.broadcasted_iota(jnp.int32, (BLK, BLK), 1)

    def kv(which, j):
        return kv_ref[pl.ds(pl.multiple_of(j * BLK, BLK), BLK), which * HD : (which + 1) * HD]

    def listed(i, s):
        s = jnp.minimum(s, counts[i] - 1)
        b = blocks[i]
        v = vis[b, jnp.maximum(s - 1, 0)]
        return jnp.where(s == 0, i, inv[jnp.where(v < b, v, vis[b, s])])

    def fold(fn, value):
        return functools.reduce(fn, [value[8 * r : 8 * r + 8] for r in range(value.shape[0] // 8)])

    blocks = [order[2 * own + i] for i in range(2)]
    counts = [count[b] for b in blocks]
    groups = [(n + GROUP - 1) // GROUP for n in counts]
    tops, totals, deltas = [], [], []

    def tiles(i, group, which):
        stored = [listed(i, group * GROUP + r) for r in range(GROUP)]
        return stored, jnp.concatenate([kv(which, j) for j in stored], axis=0)

    for i in range(2):
        at = slice(i * BLK, (i + 1) * BLK)
        for h in range(HEADS):
            q_scr[i, h * BLK : (h + 1) * BLK, :] = q_ref[at, h * HD : (h + 1) * HD]
        seg_t = jnp.broadcast_to(seg_ref[pl.ds(blocks[i], 1), :], (BLK, BLK))
        seg_u = jnp.transpose(seg_t)
        seen = (u_pos <= t_pos) & (seg_u == seg_t)
        seen = jnp.concatenate([seen.astype(F32)] * HEADS, axis=1) > 0.5
        _, keys = tiles(i, 0, 0)
        scores = nt(keys, q_scr[i])
        for r in range(GROUP):
            ok = seen if r == 0 else counts[i] > r
            part = jnp.where(ok, scores[r * BLK : (r + 1) * BLK], MASKED)
            store[i, 0, r * BLK : (r + 1) * BLK] = part
            top = fold(jnp.maximum, part) if r == 0 else jnp.maximum(top, fold(jnp.maximum, part))
        tops.append(top)
        totals.append(jnp.zeros((8, ROWS), F32))
        accum[i] = jnp.zeros((HD, ROWS), F32)

    for i in range(2):

        def score_pass(group, top, i=i):
            _, keys = tiles(i, group, 0)
            scores = nt(keys, q_scr[i])
            store[i, group] = scores
            return jnp.maximum(top, fold(jnp.maximum, scores))

        tops[i] = lax.fori_loop(1, groups[i], score_pass, tops[i])

    for i in range(2):
        tops[i] = jnp.max(tops[i], axis=0, keepdims=True)

    for i in range(2):

        def value_pass(group, total, i=i):
            lows = []
            for r in range(GROUP):
                base = jnp.where(group * GROUP + r < counts[i], tops[i], -MASKED)
                weights = jnp.exp2((store[i, group, r * BLK : (r + 1) * BLK] - base) * (SCALE * LOG2E))
                total = total + fold(jnp.add, weights)
                lows.append(weights.astype(BF))
            lows = jnp.concatenate(lows, axis=0)
            low[i, group] = lows
            _, values = tiles(i, group, 1)
            accum[i] += tn(values, lows)
            return total

        totals[i] = lax.fori_loop(0, groups[i], value_pass, totals[i])

    def grads(i, weights, values, stored):
        g = g_scr[i]
        grad = (weights.astype(F32) * (nt(values, g) - deltas[i])).astype(BF)
        grad_values = nn(weights, g)
        grad_keys = nn(grad, q_scr[i])
        for r, j in enumerate(stored):
            acc[1, j] += grad_values[r * BLK : (r + 1) * BLK]
            acc[0, j] += grad_keys[r * BLK : (r + 1) * BLK]
        return grad

    inputs[5].wait()
    eighth = jnp.full((16, HD), 0.125, BF)
    ones = jnp.ones((8, HD), BF)
    for i in range(2):
        at = slice(i * BLK, (i + 1) * BLK)
        norm = 1.0 / jnp.sum(totals[i], axis=0, keepdims=True)
        out_low = jnp.transpose((accum[i] * norm).astype(BF))
        norm = jnp.broadcast_to(norm, (8, ROWS))
        high = norm.astype(BF)
        rest_low = (norm - high.astype(F32)).astype(BF)
        norm_col = tn(jnp.concatenate([high, rest_low], axis=0), eighth)
        delta = jnp.zeros((8, ROWS), F32)
        for h in range(HEADS):
            rows = slice(h * BLK, (h + 1) * BLK)
            out_ref[at, h * HD : (h + 1) * HD] = out_low[rows]
            g = g_ref[at, h * HD : (h + 1) * HD].astype(F32)
            g_scr[i, rows, :] = (g * norm_col[rows]).astype(BF)
        g = g_scr[i].astype(F32) * out_low.astype(F32)
        high = g.astype(BF)
        rest_low = (g - high.astype(F32)).astype(BF)
        deltas.append((nt(ones, high) + nt(ones, rest_low))[0:1])
    outputs = [
        pltpu.make_async_copy(out_ref, out_any, io_sem.at[6]),
        pltpu.make_async_copy(dq_ref, dq_any, io_sem.at[7]),
    ]
    outputs[0].start()
    for i in range(2):
        accum[i] = jnp.zeros((HD, ROWS), F32)

    for i in range(2):

        def grad_pass(group, carry, i=i):
            stored, values = tiles(i, group, 1)
            _, keys = tiles(i, group, 0)
            accum[i] += tn(keys, grads(i, low[i, group], values, stored))
            return carry

        lax.fori_loop(0, groups[i], grad_pass, 0)

    for i in range(2):
        at = slice(i * BLK, (i + 1) * BLK)
        dq = jnp.transpose((accum[i] * SCALE).astype(BF))
        for h in range(HEADS):
            dq_ref[at, h * HD : (h + 1) * HD] = dq[h * BLK : (h + 1) * BLK]

    outputs[1].start()
    for ref, side, start in (
        (other_relayed_ref, 1 - core, 5),
        (mine_relayed_ref, core, 5),
        (other_ref, 1 - core, 0),
        (mine_ref, core, 0),
    ):
        for r in range(ref.shape[0]):
            at = pl.ds(16 * side + 2 * (start + r), 2)
            ref[r, :, :HD] = (acc[0, at] * SCALE).astype(BF).reshape(2 * BLK, HD)
            ref[r, :, HD:] = acc[1, at].astype(BF).reshape(2 * BLK, HD)
    for copy in outputs:
        copy.wait()


def attention(vis, count, order, query, grad_out, segments, gathered):
    vmem = pl.BlockSpec(memory_space=pltpu.VMEM)
    hbm = pl.BlockSpec(memory_space=pltpu.HBM)
    parts = [jax.ShapeDtypeStruct((n, 2 * BLK, 2 * HD), BF) for n in (len(RELAYED), len(REACHED)) for _ in range(2)]
    return pl.pallas_call(
        attention_kernel,
        in_specs=[hbm] * 6 + [vmem],
        out_specs=[hbm] * 2 + [vmem] * 4,
        out_shape=[
            jax.ShapeDtypeStruct(query.shape, BF),
            jax.ShapeDtypeStruct(query.shape, BF),
            *parts,
        ],
        scratch_shapes=[
            pltpu.VMEM((2, 24 // GROUP, GROUP * BLK, ROWS), F32),
            pltpu.VMEM((2, 24 // GROUP, GROUP * BLK, ROWS), BF),
            pltpu.VMEM((2, HD, ROWS), F32),
            pltpu.VMEM((2, ROWS, HD), BF),
            pltpu.VMEM((2, ROWS, HD), BF),
            pltpu.VMEM((2, NB, BLK, HD), F32),
            pltpu.VMEM(query.shape, BF),
            pltpu.VMEM(query.shape, BF),
            pltpu.VMEM((NB, BLK), jnp.int32),
            pltpu.VMEM(query.shape, BF),
            pltpu.VMEM(query.shape, BF),
            pltpu.SMEM(vis.shape, jnp.int32),
            pltpu.SMEM((NB,), jnp.int32),
            pltpu.SMEM((NB,), jnp.int32),
            pltpu.SMEM((NB,), jnp.int32),
            pltpu.SemaphoreType.DMA((8,)),
        ],
        compiler_params=pltpu.CompilerParams(vmem_limit_bytes=48 * 1024 * 1024),
        name="attention",
    )(vis, count, order, query, grad_out, segments, gathered)


def assemble_kernel(mine_ref, other_ref, out_ref):
    core = lax.axis_index("core")
    for y in range(4):
        for xh in range(2):
            rows = slice((2 * y + xh) * 2 * BLK, (2 * y + xh + 1) * 2 * BLK)
            for ref, which in ((mine_ref, core), (other_ref, 1 - core)):
                column = pl.multiple_of((2 * (xh * 4 + y) + which) * HD, HD)
                out_ref[:, pl.ds(column, HD)] = ref[rows, :].astype(F32)


def assemble(mine, other):
    vmem = pl.BlockSpec(memory_space=pltpu.VMEM)
    return pl.pallas_call(
        assemble_kernel,
        in_specs=[vmem] * 2,
        out_specs=vmem,
        out_shape=jax.ShapeDtypeStruct((2 * BLK, 2 * KVH * HD), F32),
        compiler_params=pltpu.CompilerParams(vmem_limit_bytes=32 * 1024 * 1024),
        name="assemble",
    )(mine, other)


def wide(*parts):
    return functools.reduce(jnp.add, [p.astype(F32) for p in parts])


def shards(query, keyval, grad_out, vis_blocks, vis_count, segment_ids, block_order):
    xh, y, core = (lax.axis_index(a) for a in ("xh", "y", "core"))
    first = core == 0

    def across(value, by):
        pairs = [
            ((a * 8 + i) * 2 + c, ((a ^ c) * 8 + (i + by) % 8) * 2 + c)
            for a in range(2)
            for i in range(8)
            for c in range(2)
        ]
        return lax.ppermute(value, ("x", "z", "core"), pairs)

    def halves(value):
        return jnp.where(first, value[:, :HD], value[:, HD:]), jnp.where(first, value[:, HD:], value[:, :HD])

    near = lax.dynamic_slice_in_dim(keyval, (xh * 4 + y) * 2 * HD, 2 * HD, 1)
    up2, down2 = across(near, 2), across(near, -2)
    up1, down1 = across(near, 1), across(near, -1)
    own = across(near, 0)
    up3, down3 = shift(up2, "z", 8, 1), shift(down2, "z", 8, -1)
    up4, down4 = shift(up2[:BLK], "z", 8, 2), shift(down2[BLK:], "z", 8, -2)
    reached = jnp.concatenate([own, down1, down2, up2, up1], axis=0)
    relayed = jnp.concatenate([down3, up4, down4, up3], axis=0)
    sides = [(mine, swap(mine, "core")) for mine in (reached, relayed)]
    gathered = [jnp.where(first, mine, other) for mine, other in sides]
    gathered = jnp.concatenate(gathered + [jnp.where(first, other, mine) for mine, other in sides], axis=0)
    inputs = (vis_blocks, vis_count, block_order, query, grad_out, segment_ids.reshape(NB, BLK))
    inputs = [pltpu.with_memory_space_constraint(v, pltpu.HBM) for v in inputs]
    attn_out, grad_query, other_relayed, mine_relayed, other, mine = attention(
        *inputs, gathered
    )
    relayed = wide(mine_relayed, swap(other_relayed, "core")).astype(BF)
    reached = wide(mine, swap(other, "core")).astype(BF)
    joined = dict(zip(RELAYED + REACHED, [relayed[k] for k in range(3)] + [reached[k] for k in range(5)]))
    for4_up, for4_down = shift(joined[4][:BLK], "z", 8, 2), shift(joined[4][BLK:], "z", 8, -2)
    for3_up, for3_down = shift(joined[3], "z", 8, 1), shift(joined[5], "z", 8, -1)
    up2 = jnp.concatenate(
        [wide(joined[2][:BLK], for3_up[:BLK], for4_up), wide(joined[2][BLK:], for3_up[BLK:])], axis=0
    )
    down2 = jnp.concatenate(
        [wide(joined[6][:BLK], for3_down[:BLK]), wide(joined[6][BLK:], for3_down[BLK:], for4_down)], axis=0
    )
    for2_up, for2_down = across(up2.astype(BF), 2), across(down2.astype(BF), -2)
    for1_up, for1_down = across(joined[1], 1), across(joined[7], -1)
    own = across(joined[0], 0)
    kept, given = halves(wide(own, for1_up, for1_down, for2_up, for2_down))
    summed = wide(kept, swap(given.astype(BF), "core")).astype(BF)
    mine = lax.all_to_all(jnp.concatenate([summed] * KVH, axis=0), ("y", "xh"), 0, 0, tiled=True)
    return attn_out, grad_query, assemble(mine, swap(mine, "core"))


def solution(mesh):
    fine = Mesh(mesh.devices.reshape(2, 8, 2, 4, 2), ("x", "z", "xh", "y", "core"))
    ctx, head = ("x", "z"), ("xh", "y", "core")
    return jax.shard_map(
        shards,
        mesh=fine,
        in_specs=(P(ctx, head), P(ctx, None), P(ctx, head), P(), P(), P(), P()),
        out_specs=(P(ctx, head), P(ctx, head), P(ctx, None)),
        check_vma=False,
    )
```

```python
import functools

import jax
import jax.numpy as jnp
from jax import lax
from jax.experimental import pallas as pl
from jax.experimental.pallas import tpu as pltpu
from jax.sharding import Mesh, PartitionSpec as P

QH = 64
KVH = 8
HD = 128
BLK = 128
NB = 32
HEADS = 4
GROUP = 8
REACHED = (0, 1, 2, 6, 7)
RELAYED = (3, 4, 5)
ROWS = HEADS * BLK
SCALE = HD**-0.5
LOG2E = 1.4426950408889634
MASKED = -1e30
BF = jnp.bfloat16
F32 = jnp.float32


def shift(value, axis, size, by):
    return lax.ppermute(value, axis, [(i, (i + by) % size) for i in range(size)])


def swap(value, axis):
    return lax.ppermute(value, axis, [(0, 1), (1, 0)])


def nt(a, b):
    return lax.dot_general(a, b, (((1,), (1,)), ((), ())), preferred_element_type=F32)


def nn(a, b):
    return lax.dot_general(a, b, (((1,), (0,)), ((), ())), preferred_element_type=F32)


def tn(a, b):
    return lax.dot_general(a, b, (((0,), (0,)), ((), ())), preferred_element_type=F32)


def attention_kernel(
    vis_any, count_any, order_any, q_any, g_any, seg_any, kv_ref,
    out_any, dq_any, other_relayed_ref, mine_relayed_ref, other_ref, mine_ref,
    store, low, accum, q_scr, g_scr, acc, q_ref, g_ref, seg_ref, out_ref, dq_ref,
    vis, count, order, inv, io_sem,
):
    x, z, core = lax.axis_index("x"), lax.axis_index("z"), lax.axis_index("core")
    own = x * 8 + z
    pairs = [
        (order_any, order),
        (count_any, count),
        (vis_any, vis),
        (q_any, q_ref),
        (seg_any, seg_ref),
        (g_any, g_ref),
    ]
    inputs = [pltpu.make_async_copy(*pair, io_sem.at[k]) for k, pair in enumerate(pairs)]
    for copy in inputs:
        copy.start()
    acc[...] = jnp.zeros_like(acc)
    inputs[0].wait()

    def place(j, carry):
        shard = j // 2
        by_z = lax.rem(shard - z + 16, 8)
        at = jnp.where(by_z < 3, by_z, jnp.where(by_z > 5, by_z - 3, by_z + 2))
        inv[order[j]] = jnp.where(shard // 8 == x, 0, 16) + 2 * at + lax.rem(j, 2)
        return carry

    lax.fori_loop(0, NB, place, 0, unroll=True)
    for copy in inputs[1:5]:
        copy.wait()

    u_pos = lax.broadcasted_iota(jnp.int32, (BLK, BLK), 0)
    t_pos = lax.broadcasted_iota(jnp.int32, (BLK, BLK), 1)

    def kv(which, j):
        return kv_ref[pl.ds(pl.multiple_of(j * BLK, BLK), BLK), which * HD : (which + 1) * HD]

    def listed(i, s):
        s = jnp.minimum(s, counts[i] - 1)
        b = blocks[i]
        v = vis[b, jnp.maximum(s - 1, 0)]
        return jnp.where(s == 0, i, inv[jnp.where(v < b, v, vis[b, s])])

    def fold(fn, value):
        return functools.reduce(fn, [value[8 * r : 8 * r + 8] for r in range(value.shape[0] // 8)])

    blocks = [order[2 * own + i] for i in range(2)]
    counts = [count[b] for b in blocks]
    groups = [(n + GROUP - 1) // GROUP for n in counts]
    tops, totals, deltas = [], [], []

    def tiles(i, group, which):
        stored = [listed(i, group * GROUP + r) for r in range(GROUP)]
        return stored, jnp.concatenate([kv(which, j) for j in stored], axis=0)

    for i in range(2):
        at = slice(i * BLK, (i + 1) * BLK)
        for h in range(HEADS):
            q_scr[i, h * BLK : (h + 1) * BLK, :] = q_ref[at, h * HD : (h + 1) * HD]
        seg_t = jnp.broadcast_to(seg_ref[pl.ds(blocks[i], 1), :], (BLK, BLK))
        seg_u = jnp.transpose(seg_t)
        seen = (u_pos <= t_pos) & (seg_u == seg_t)
        seen = jnp.concatenate([seen.astype(F32)] * HEADS, axis=1) > 0.5
        _, keys = tiles(i, 0, 0)
        scores = nt(keys, q_scr[i])
        for r in range(GROUP):
            ok = seen if r == 0 else counts[i] > r
            part = jnp.where(ok, scores[r * BLK : (r + 1) * BLK], MASKED)
            store[i, 0, r * BLK : (r + 1) * BLK] = part
            top = fold(jnp.maximum, part) if r == 0 else jnp.maximum(top, fold(jnp.maximum, part))
        tops.append(top)
        totals.append(jnp.zeros((8, ROWS), F32))
        accum[i] = jnp.zeros((HD, ROWS), F32)

    for i in range(2):

        def score_pass(group, top, i=i):
            _, keys = tiles(i, group, 0)
            scores = nt(keys, q_scr[i])
            store[i, group] = scores
            return jnp.maximum(top, fold(jnp.maximum, scores))

        tops[i] = lax.fori_loop(1, groups[i], score_pass, tops[i])

    for i in range(2):
        tops[i] = jnp.max(tops[i], axis=0, keepdims=True)

    for i in range(2):

        def value_pass(group, total, i=i):
            lows = []
            for r in range(GROUP):
                base = jnp.where(group * GROUP + r < counts[i], tops[i], -MASKED)
                weights = jnp.exp2((store[i, group, r * BLK : (r + 1) * BLK] - base) * (SCALE * LOG2E))
                total = total + fold(jnp.add, weights)
                lows.append(weights.astype(BF))
            lows = jnp.concatenate(lows, axis=0)
            low[i, group] = lows
            _, values = tiles(i, group, 1)
            accum[i] += tn(values, lows)
            return total

        totals[i] = lax.fori_loop(0, groups[i], value_pass, totals[i])

    def grads(i, weights, values, stored):
        g = g_scr[i]
        grad = (weights.astype(F32) * (nt(values, g) - deltas[i])).astype(BF)
        grad_values = nn(weights, g)
        grad_keys = nn(grad, q_scr[i])
        for r, j in enumerate(stored):
            acc[1, j] += grad_values[r * BLK : (r + 1) * BLK]
            acc[0, j] += grad_keys[r * BLK : (r + 1) * BLK]
        return grad

    inputs[5].wait()
    eighth = jnp.full((16, HD), 0.125, BF)
    ones = jnp.ones((8, HD), BF)
    for i in range(2):
        at = slice(i * BLK, (i + 1) * BLK)
        norm = 1.0 / jnp.sum(totals[i], axis=0, keepdims=True)
        out_low = jnp.transpose((accum[i] * norm).astype(BF))
        norm = jnp.broadcast_to(norm, (8, ROWS))
        high = norm.astype(BF)
        rest_low = (norm - high.astype(F32)).astype(BF)
        norm_col = tn(jnp.concatenate([high, rest_low], axis=0), eighth)
        for h in range(HEADS):
            rows = slice(h * BLK, (h + 1) * BLK)
            out_ref[at, h * HD : (h + 1) * HD] = out_low[rows]
            g = g_ref[at, h * HD : (h + 1) * HD].astype(F32)
            g_scr[i, rows, :] = (g * norm_col[rows]).astype(BF)
        g = g_scr[i].astype(F32) * out_low.astype(F32)
        high = g.astype(BF)
        rest_low = (g - high.astype(F32)).astype(BF)
        deltas.append((nt(ones, high) + nt(ones, rest_low))[0:1])
    outputs = [
        pltpu.make_async_copy(out_ref, out_any, io_sem.at[6]),
        *[
            pltpu.make_async_copy(
                dq_ref.at[pl.ds(i * BLK, BLK)], dq_any.at[pl.ds(i * BLK, BLK)], io_sem.at[7 + i]
            )
            for i in range(2)
        ],
    ]
    outputs[0].start()
    for i in range(2):
        accum[i] = jnp.zeros((HD, ROWS), F32)

    for i in range(2):

        def grad_pass(group, carry, i=i):
            stored, values = tiles(i, group, 1)
            _, keys = tiles(i, group, 0)
            accum[i] += tn(keys, grads(i, low[i, group], values, stored))
            return carry

        lax.fori_loop(0, groups[i], grad_pass, 0)
        at = slice(i * BLK, (i + 1) * BLK)
        dq = jnp.transpose((accum[i] * SCALE).astype(BF))
        for h in range(HEADS):
            dq_ref[at, h * HD : (h + 1) * HD] = dq[h * BLK : (h + 1) * BLK]
        outputs[1 + i].start()

    for ref, side, start in (
        (other_relayed_ref, 1 - core, 5),
        (mine_relayed_ref, core, 5),
        (other_ref, 1 - core, 0),
        (mine_ref, core, 0),
    ):
        for r in range(ref.shape[0]):
            at = pl.ds(16 * side + 2 * (start + r), 2)
            ref[r, :, :HD] = (acc[0, at] * SCALE).astype(BF).reshape(2 * BLK, HD)
            ref[r, :, HD:] = acc[1, at].astype(BF).reshape(2 * BLK, HD)
    for copy in outputs:
        copy.wait()


def attention(vis, count, order, query, grad_out, segments, gathered):
    vmem = pl.BlockSpec(memory_space=pltpu.VMEM)
    hbm = pl.BlockSpec(memory_space=pltpu.HBM)
    parts = [jax.ShapeDtypeStruct((n, 2 * BLK, 2 * HD), BF) for n in (len(RELAYED), len(REACHED)) for _ in range(2)]
    return pl.pallas_call(
        attention_kernel,
        in_specs=[hbm] * 6 + [vmem],
        out_specs=[hbm] * 2 + [vmem] * 4,
        out_shape=[
            jax.ShapeDtypeStruct(query.shape, BF),
            jax.ShapeDtypeStruct(query.shape, BF),
            *parts,
        ],
        scratch_shapes=[
            pltpu.VMEM((2, 24 // GROUP, GROUP * BLK, ROWS), F32),
            pltpu.VMEM((2, 24 // GROUP, GROUP * BLK, ROWS), BF),
            pltpu.VMEM((2, HD, ROWS), F32),
            pltpu.VMEM((2, ROWS, HD), BF),
            pltpu.VMEM((2, ROWS, HD), BF),
            pltpu.VMEM((2, NB, BLK, HD), F32),
            pltpu.VMEM(query.shape, BF),
            pltpu.VMEM(query.shape, BF),
            pltpu.VMEM((NB, BLK), jnp.int32),
            pltpu.VMEM(query.shape, BF),
            pltpu.VMEM(query.shape, BF),
            pltpu.SMEM(vis.shape, jnp.int32),
            pltpu.SMEM((NB,), jnp.int32),
            pltpu.SMEM((NB,), jnp.int32),
            pltpu.SMEM((NB,), jnp.int32),
            pltpu.SemaphoreType.DMA((9,)),
        ],
        compiler_params=pltpu.CompilerParams(vmem_limit_bytes=48 * 1024 * 1024),
        name="attention",
    )(vis, count, order, query, grad_out, segments, gathered)


def assemble_kernel(mine_ref, other_ref, out_ref):
    core = lax.axis_index("core")
    for y in range(4):
        for xh in range(2):
            rows = slice((2 * y + xh) * 2 * BLK, (2 * y + xh + 1) * 2 * BLK)
            for ref, which in ((mine_ref, core), (other_ref, 1 - core)):
                column = pl.multiple_of((2 * (xh * 4 + y) + which) * HD, HD)
                out_ref[:, pl.ds(column, HD)] = ref[rows, :].astype(F32)


def assemble(mine, other):
    vmem = pl.BlockSpec(memory_space=pltpu.VMEM)
    return pl.pallas_call(
        assemble_kernel,
        in_specs=[vmem] * 2,
        out_specs=vmem,
        out_shape=jax.ShapeDtypeStruct((2 * BLK, 2 * KVH * HD), F32),
        compiler_params=pltpu.CompilerParams(vmem_limit_bytes=32 * 1024 * 1024),
        name="assemble",
    )(mine, other)


def wide(*parts):
    return functools.reduce(jnp.add, [p.astype(F32) for p in parts])


def shards(query, keyval, grad_out, vis_blocks, vis_count, segment_ids, block_order):
    xh, y, core = (lax.axis_index(a) for a in ("xh", "y", "core"))
    first = core == 0

    def across(value, by):
        pairs = [
            ((a * 8 + i) * 2 + c, ((a ^ c) * 8 + (i + by) % 8) * 2 + c)
            for a in range(2)
            for i in range(8)
            for c in range(2)
        ]
        return lax.ppermute(value, ("x", "z", "core"), pairs)

    def halves(value):
        return jnp.where(first, value[:, :HD], value[:, HD:]), jnp.where(first, value[:, HD:], value[:, :HD])

    near = lax.dynamic_slice_in_dim(keyval, (xh * 4 + y) * 2 * HD, 2 * HD, 1)
    up2, down2 = across(near, 2), across(near, -2)
    up1, down1 = across(near, 1), across(near, -1)
    own = across(near, 0)
    up3, down3 = shift(up2, "z", 8, 1), shift(down2, "z", 8, -1)
    up4, down4 = shift(up2[:BLK], "z", 8, 2), shift(down2[BLK:], "z", 8, -2)
    reached = jnp.concatenate([own, down1, down2, up2, up1], axis=0)
    relayed = jnp.concatenate([down3, up4, down4, up3], axis=0)
    sides = [(mine, swap(mine, "core")) for mine in (reached, relayed)]
    gathered = [jnp.where(first, mine, other) for mine, other in sides]
    gathered = jnp.concatenate(gathered + [jnp.where(first, other, mine) for mine, other in sides], axis=0)
    inputs = (vis_blocks, vis_count, block_order, query, grad_out, segment_ids.reshape(NB, BLK))
    inputs = [pltpu.with_memory_space_constraint(v, pltpu.HBM) for v in inputs]
    attn_out, grad_query, other_relayed, mine_relayed, other, mine = attention(
        *inputs, gathered
    )
    relayed = wide(mine_relayed, swap(other_relayed, "core")).astype(BF)
    reached = wide(mine, swap(other, "core")).astype(BF)
    joined = dict(zip(RELAYED + REACHED, [relayed[k] for k in range(3)] + [reached[k] for k in range(5)]))
    for4_up, for4_down = shift(joined[4][:BLK], "z", 8, 2), shift(joined[4][BLK:], "z", 8, -2)
    for3_up, for3_down = shift(joined[3], "z", 8, 1), shift(joined[5], "z", 8, -1)
    up2 = jnp.concatenate(
        [wide(joined[2][:BLK], for3_up[:BLK], for4_up), wide(joined[2][BLK:], for3_up[BLK:])], axis=0
    )
    down2 = jnp.concatenate(
        [wide(joined[6][:BLK], for3_down[:BLK]), wide(joined[6][BLK:], for3_down[BLK:], for4_down)], axis=0
    )
    for2_up, for2_down = across(up2.astype(BF), 2), across(down2.astype(BF), -2)
    for1_up, for1_down = across(joined[1], 1), across(joined[7], -1)
    own = across(joined[0], 0)
    kept, given = halves(wide(own, for1_up, for1_down, for2_up, for2_down))
    summed = wide(kept, swap(given.astype(BF), "core")).astype(BF)
    mine = lax.all_to_all(jnp.concatenate([summed] * KVH, axis=0), ("y", "xh"), 0, 0, tiled=True)
    return attn_out, grad_query, assemble(mine, swap(mine, "core"))


def solution(mesh):
    fine = Mesh(mesh.devices.reshape(2, 8, 2, 4, 2), ("x", "z", "xh", "y", "core"))
    ctx, head = ("x", "z"), ("xh", "y", "core")
    return jax.shard_map(
        shards,
        mesh=fine,
        in_specs=(P(ctx, head), P(ctx, None), P(ctx, head), P(), P(), P(), P()),
        out_specs=(P(ctx, head), P(ctx, head), P(ctx, None)),
        check_vma=False,
    )
```

```python
import functools

import jax
import jax.numpy as jnp
from jax import lax
from jax.experimental import pallas as pl
from jax.experimental.pallas import tpu as pltpu
from jax.sharding import Mesh, PartitionSpec as P

QH = 64
KVH = 8
HD = 128
BLK = 128
NB = 32
HEADS = 4
GROUP = 8
REACHED = (0, 1, 2, 6, 7)
RELAYED = (3, 4, 5)
ROWS = HEADS * BLK
SCALE = HD**-0.5
LOG2E = 1.4426950408889634
MASKED = -1e30
BF = jnp.bfloat16
F32 = jnp.float32


def shift(value, axis, size, by):
    return lax.ppermute(value, axis, [(i, (i + by) % size) for i in range(size)])


def swap(value, axis):
    return lax.ppermute(value, axis, [(0, 1), (1, 0)])


def nt(a, b):
    return lax.dot_general(a, b, (((1,), (1,)), ((), ())), preferred_element_type=F32)


def nn(a, b):
    return lax.dot_general(a, b, (((1,), (0,)), ((), ())), preferred_element_type=F32)


def tn(a, b):
    return lax.dot_general(a, b, (((0,), (0,)), ((), ())), preferred_element_type=F32)


def attention_kernel(
    vis_any, count_any, order_any, q_any, g_any, seg_any, kv_ref,
    out_any, dq_any, other_relayed_ref, mine_relayed_ref, other_ref, mine_ref,
    store, low, accum, q_scr, g_scr, acc, q_ref, g_ref, seg_ref, out_ref, dq_ref,
    vis, count, order, inv, io_sem,
):
    x, z, core = lax.axis_index("x"), lax.axis_index("z"), lax.axis_index("core")
    own = x * 8 + z
    pairs = [
        (order_any, order),
        (count_any, count),
        (vis_any, vis),
        (q_any, q_ref),
        (seg_any, seg_ref),
        (g_any, g_ref),
    ]
    inputs = [pltpu.make_async_copy(*pair, io_sem.at[k]) for k, pair in enumerate(pairs)]
    for copy in inputs:
        copy.start()
    acc[...] = jnp.zeros_like(acc)
    inputs[0].wait()

    def place(j, carry):
        shard = j // 2
        by_z = lax.rem(shard - z + 16, 8)
        at = jnp.where(by_z < 3, by_z, jnp.where(by_z > 5, by_z - 3, by_z + 2))
        inv[order[j]] = jnp.where(shard // 8 == x, 0, 16) + 2 * at + lax.rem(j, 2)
        return carry

    lax.fori_loop(0, NB, place, 0, unroll=True)
    for copy in inputs[1:5]:
        copy.wait()

    u_pos = lax.broadcasted_iota(jnp.int32, (BLK, BLK), 0)
    t_pos = lax.broadcasted_iota(jnp.int32, (BLK, BLK), 1)

    def kv(which, j):
        return kv_ref[pl.ds(pl.multiple_of(j * BLK, BLK), BLK), which * HD : (which + 1) * HD]

    def listed(i, s):
        s = jnp.minimum(s, counts[i] - 1)
        b = blocks[i]
        v = vis[b, jnp.maximum(s - 1, 0)]
        return jnp.where(s == 0, i, inv[jnp.where(v < b, v, vis[b, s])])

    def fold(fn, value):
        return functools.reduce(fn, [value[8 * r : 8 * r + 8] for r in range(value.shape[0] // 8)])

    blocks = [order[2 * own + i] for i in range(2)]
    counts = [count[b] for b in blocks]
    groups = [(n + GROUP - 1) // GROUP for n in counts]
    tops, totals, deltas = [], [], []

    def tiles(i, group, which):
        stored = [listed(i, group * GROUP + r) for r in range(GROUP)]
        return stored, jnp.concatenate([kv(which, j) for j in stored], axis=0)

    for i in range(2):
        at = slice(i * BLK, (i + 1) * BLK)
        for h in range(HEADS):
            q_scr[i, h * BLK : (h + 1) * BLK, :] = q_ref[at, h * HD : (h + 1) * HD]
        seg_t = jnp.broadcast_to(seg_ref[pl.ds(blocks[i], 1), :], (BLK, BLK))
        seg_u = jnp.transpose(seg_t)
        seen = (u_pos <= t_pos) & (seg_u == seg_t)
        seen = jnp.concatenate([seen.astype(F32)] * HEADS, axis=1) > 0.5
        _, keys = tiles(i, 0, 0)
        scores = nt(keys, q_scr[i])
        for r in range(GROUP):
            ok = seen if r == 0 else counts[i] > r
            part = jnp.where(ok, scores[r * BLK : (r + 1) * BLK], MASKED)
            store[i, 0, r * BLK : (r + 1) * BLK] = part
            top = fold(jnp.maximum, part) if r == 0 else jnp.maximum(top, fold(jnp.maximum, part))
        tops.append(top)
        totals.append(jnp.zeros((8, ROWS), F32))
        accum[i] = jnp.zeros((HD, ROWS), F32)

    for i in range(2):

        def score_pass(group, top, i=i):
            _, keys = tiles(i, group, 0)
            scores = nt(keys, q_scr[i])
            store[i, group] = scores
            return jnp.maximum(top, fold(jnp.maximum, scores))

        tops[i] = lax.fori_loop(1, groups[i], score_pass, tops[i])

    for i in range(2):
        tops[i] = jnp.max(tops[i], axis=0, keepdims=True)

    for i in range(2):

        def value_pass(group, total, i=i):
            lows = []
            for r in range(GROUP):
                base = jnp.where(group * GROUP + r < counts[i], tops[i], -MASKED)
                weights = jnp.exp2((store[i, group, r * BLK : (r + 1) * BLK] - base) * (SCALE * LOG2E))
                total = total + fold(jnp.add, weights)
                lows.append(weights.astype(BF))
            lows = jnp.concatenate(lows, axis=0)
            low[i, group] = lows
            _, values = tiles(i, group, 1)
            accum[i] += tn(values, lows)
            return total

        totals[i] = lax.fori_loop(0, groups[i], value_pass, totals[i])

    def grads(i, weights, values, stored):
        g = g_scr[i]
        grad = (weights.astype(F32) * (nt(values, g) - deltas[i])).astype(BF)
        grad_values = nn(weights, g)
        grad_keys = nn(grad, q_scr[i])
        for r, j in enumerate(stored):
            acc[1, j] += grad_values[r * BLK : (r + 1) * BLK]
            acc[0, j] += grad_keys[r * BLK : (r + 1) * BLK]
        return grad

    inputs[5].wait()
    eighth = jnp.full((16, HD), 0.125, BF)
    ones = jnp.ones((8, HD), BF)
    for i in range(2):
        at = slice(i * BLK, (i + 1) * BLK)
        norm = 1.0 / jnp.sum(totals[i], axis=0, keepdims=True)
        out_low = jnp.transpose((accum[i] * norm).astype(BF))
        norm = jnp.broadcast_to(norm, (8, ROWS))
        high = norm.astype(BF)
        rest_low = (norm - high.astype(F32)).astype(BF)
        norm_col = tn(jnp.concatenate([high, rest_low], axis=0), eighth)
        for h in range(HEADS):
            rows = slice(h * BLK, (h + 1) * BLK)
            out_ref[at, h * HD : (h + 1) * HD] = out_low[rows]
            g = g_ref[at, h * HD : (h + 1) * HD].astype(F32)
            g_scr[i, rows, :] = (g * norm_col[rows]).astype(BF)
        g = g_scr[i].astype(F32) * out_low.astype(F32)
        high = g.astype(BF)
        rest_low = (g - high.astype(F32)).astype(BF)
        deltas.append((nt(ones, high) + nt(ones, rest_low))[0:1])
    outputs = [
        pltpu.make_async_copy(out_ref, out_any, io_sem.at[6]),
        *[
            pltpu.make_async_copy(
                dq_ref.at[pl.ds(i * BLK, BLK)], dq_any.at[pl.ds(i * BLK, BLK)], io_sem.at[7 + i]
            )
            for i in range(2)
        ],
    ]
    outputs[0].start()
    for i in range(2):
        accum[i] = jnp.zeros((HD, ROWS), F32)

    for i in range(2):

        def grad_pass(group, carry, i=i):
            stored, values = tiles(i, group, 1)
            _, keys = tiles(i, group, 0)
            accum[i] += tn(keys, grads(i, low[i, group], values, stored))
            return carry

        lax.fori_loop(0, groups[i], grad_pass, 0)
        at = slice(i * BLK, (i + 1) * BLK)
        dq = jnp.transpose((accum[i] * SCALE).astype(BF))
        for h in range(HEADS):
            dq_ref[at, h * HD : (h + 1) * HD] = dq[h * BLK : (h + 1) * BLK]
        outputs[1 + i].start()

    for ref, side, start in (
        (other_relayed_ref, 1 - core, 5),
        (mine_relayed_ref, core, 5),
        (other_ref, 1 - core, 0),
        (mine_ref, core, 0),
    ):
        for r in range(ref.shape[0]):
            at = pl.ds(16 * side + 2 * (start + r), 2)
            ref[r, :, :HD] = (acc[0, at] * SCALE).astype(BF).reshape(2 * BLK, HD)
            ref[r, :, HD:] = acc[1, at].astype(BF).reshape(2 * BLK, HD)
    for copy in outputs:
        copy.wait()


def attention(vis, count, order, query, grad_out, segments, gathered):
    vmem = pl.BlockSpec(memory_space=pltpu.VMEM)
    hbm = pl.BlockSpec(memory_space=pltpu.HBM)
    parts = [jax.ShapeDtypeStruct((n, 2 * BLK, 2 * HD), BF) for n in (len(RELAYED), len(REACHED)) for _ in range(2)]
    return pl.pallas_call(
        attention_kernel,
        in_specs=[hbm] * 6 + [vmem],
        out_specs=[hbm] * 2 + [vmem] * 4,
        out_shape=[
            jax.ShapeDtypeStruct(query.shape, BF),
            jax.ShapeDtypeStruct(query.shape, BF),
            *parts,
        ],
        scratch_shapes=[
            pltpu.VMEM((2, 24 // GROUP, GROUP * BLK, ROWS), F32),
            pltpu.VMEM((2, 24 // GROUP, GROUP * BLK, ROWS), BF),
            pltpu.VMEM((2, HD, ROWS), F32),
            pltpu.VMEM((2, ROWS, HD), BF),
            pltpu.VMEM((2, ROWS, HD), BF),
            pltpu.VMEM((2, NB, BLK, HD), F32),
            pltpu.VMEM(query.shape, BF),
            pltpu.VMEM(query.shape, BF),
            pltpu.VMEM((NB, BLK), jnp.int32),
            pltpu.VMEM(query.shape, BF),
            pltpu.VMEM(query.shape, BF),
            pltpu.SMEM(vis.shape, jnp.int32),
            pltpu.SMEM((NB,), jnp.int32),
            pltpu.SMEM((NB,), jnp.int32),
            pltpu.SMEM((NB,), jnp.int32),
            pltpu.SemaphoreType.DMA((9,)),
        ],
        compiler_params=pltpu.CompilerParams(vmem_limit_bytes=48 * 1024 * 1024),
        name="attention",
    )(vis, count, order, query, grad_out, segments, gathered)


def assemble_kernel(mine_ref, other_ref, out_ref):
    core = lax.axis_index("core")
    for y in range(4):
        for xh in range(2):
            rows = slice((2 * y + xh) * 2 * BLK, (2 * y + xh + 1) * 2 * BLK)
            for ref, which in ((mine_ref, core), (other_ref, 1 - core)):
                column = pl.multiple_of((2 * (xh * 4 + y) + which) * HD, HD)
                out_ref[:, pl.ds(column, HD)] = ref[rows, :].astype(F32)


def assemble(mine, other):
    vmem = pl.BlockSpec(memory_space=pltpu.VMEM)
    return pl.pallas_call(
        assemble_kernel,
        in_specs=[vmem] * 2,
        out_specs=vmem,
        out_shape=jax.ShapeDtypeStruct((2 * BLK, 2 * KVH * HD), F32),
        compiler_params=pltpu.CompilerParams(vmem_limit_bytes=32 * 1024 * 1024),
        name="assemble",
    )(mine, other)


def wide(*parts):
    return functools.reduce(jnp.add, [p.astype(F32) for p in parts])


def shards(query, keyval, grad_out, vis_blocks, vis_count, segment_ids, block_order):
    xh, y, core = (lax.axis_index(a) for a in ("xh", "y", "core"))
    first = core == 0

    def across(value, by):
        pairs = [
            ((a * 8 + i) * 2 + c, ((a ^ c) * 8 + (i + by) % 8) * 2 + c)
            for a in range(2)
            for i in range(8)
            for c in range(2)
        ]
        return lax.ppermute(value, ("x", "z", "core"), pairs)

    def split(value, by):
        pairs = [(2 * i + c, 2 * ((i + (by, -by)[c]) % 8) + c) for i in range(8) for c in range(2)]
        return lax.ppermute(value, ("z", "core"), pairs)

    def halves(value):
        return jnp.where(first, value[:, :HD], value[:, HD:]), jnp.where(first, value[:, HD:], value[:, :HD])

    near = lax.dynamic_slice_in_dim(keyval, (xh * 4 + y) * 2 * HD, 2 * HD, 1)
    up2, down2 = across(near, 2), across(near, -2)
    up1, down1 = across(near, 1), across(near, -1)
    own = across(near, 0)
    up3, down3 = shift(up2, "z", 8, 1), shift(down2, "z", 8, -1)
    up4, down4 = shift(up2[:BLK], "z", 8, 2), shift(down2[BLK:], "z", 8, -2)
    reached = jnp.concatenate([own, down1, down2, up2, up1], axis=0)
    relayed = jnp.concatenate([down3, up4, down4, up3], axis=0)
    sides = [(mine, swap(mine, "core")) for mine in (reached, relayed)]
    gathered = [jnp.where(first, mine, other) for mine, other in sides]
    gathered = jnp.concatenate(gathered + [jnp.where(first, other, mine) for mine, other in sides], axis=0)
    inputs = (vis_blocks, vis_count, block_order, query, grad_out, segment_ids.reshape(NB, BLK))
    inputs = [pltpu.with_memory_space_constraint(v, pltpu.HBM) for v in inputs]
    attn_out, grad_query, other_relayed, mine_relayed, other, mine = attention(
        *inputs, gathered
    )
    relayed = wide(mine_relayed, swap(other_relayed, "core")).astype(BF)
    reached = wide(mine, swap(other, "core")).astype(BF)
    joined = dict(zip(RELAYED + REACHED, [relayed[k] for k in range(3)] + [reached[k] for k in range(5)]))
    for4 = split(joined[4], 2)
    for3_up, for3_down = shift(joined[3], "z", 8, 1), shift(joined[5], "z", 8, -1)
    zero = jnp.zeros_like(for4)
    up2 = wide(joined[2], for3_up, jnp.where(first, for4, zero))
    down2 = wide(joined[6], for3_down, jnp.where(first, zero, for4))
    for2_up, for2_down = across(up2.astype(BF), 2), across(down2.astype(BF), -2)
    for1_up, for1_down = across(joined[1], 1), across(joined[7], -1)
    own = across(joined[0], 0)
    kept, given = halves(wide(own, for1_up, for1_down, for2_up, for2_down))
    summed = wide(kept, swap(given.astype(BF), "core")).astype(BF)
    mine = lax.all_to_all(jnp.concatenate([summed] * KVH, axis=0), ("y", "xh"), 0, 0, tiled=True)
    return attn_out, grad_query, assemble(mine, swap(mine, "core"))


def solution(mesh):
    fine = Mesh(mesh.devices.reshape(2, 8, 2, 4, 2), ("x", "z", "xh", "y", "core"))
    ctx, head = ("x", "z"), ("xh", "y", "core")
    return jax.shard_map(
        shards,
        mesh=fine,
        in_specs=(P(ctx, head), P(ctx, None), P(ctx, head), P(), P(), P(), P()),
        out_specs=(P(ctx, head), P(ctx, head), P(ctx, None)),
        check_vma=False,
    )
```
